512 devices in a mesh: lon: 32 (over z_lo, y, core), lat: 16 (over x, z_hi).
Axes of the slice: x: 4, y: 8, z: 8 (z_hi: 4, z_lo: 2; z = z_hi * 2 + z_lo), core: 2. Of those that a mesh axis runs over, the one named last changes fastest.
Arguments:
- thermal_anomaly: float32 [46, 128, 4096], P(None, 'lat', 'lon'), may hold values from -6 to 6
- saltiness_anomaly: float32 [46, 128, 4096], P(None, 'lat', 'lon'), may hold values from -6 to 6
- zonal_volume_flux: float32 [46, 128, 4096], P(None, 'lat', 'lon'), may hold values from -0.2 to 0.2
- meridional_volume_flux: float32 [46, 128, 4096], P(None, 'lat', 'lon'), may hold values from -0.2 to 0.2
- vertical_diffusion_factor: float32 [46, 128, 4096], P(None, 'lat', 'lon'), may hold values from 0.05 to 5
- friction_factor: float32 [46, 128, 4096], P(None, 'lat', 'lon'), may hold values from 0.1 to 3
- seawater_indicator: int32 [128, 4096], P('lat', 'lon'), may hold values 0 or 1
- water_layer_depth: int32 [128, 4096], P('lat', 'lon'), may hold values from 1 to 46
Outputs:
- temperature_next: float32 [46, 128, 4096], P(None, 'lat', 'lon')
- salinity_next: float32 [46, 128, 4096], P(None, 'lat', 'lon')
The draws below stay inside these ranges and needn't reach their ends.
All inputs are finite; a program needn't handle non-finite values. No bound on the sum of `seawater_indicator` on one device may be relied on, other than what follows from the above.
Results may differ from the reference program's by a relative error of at most 0.00002.
Values sent between devices are 32-bit elements; how exact they have to be, the bound alone decides.
No kernel may reach another device: no remote copies, remote signals or barrier semaphores. Data moves between devices by JAX's collectives and lax.ppermute only.
A program may use at most 64 MiB of HBM per device.

```python
import math
import jax
import jax.numpy as jnp

DEPTH_LAYERS = 46
SPLIT_PASSES = 4
MERIDIAN_NUMBER = 4096
PARALLEL_NUMBER = 128


def plant(result, key, least, largest):
    longest = result.shape.index(max(result.shape))
    spots = []
    for shift in (0, 1):
        where = [jax.random.randint(jax.random.fold_in(key, axis), (), 0, length) for axis, length in enumerate(result.shape)]
        where[longest] = (where[longest] + shift) % result.shape[longest]
        spots.append(tuple(where))
    return result.at[spots[0]].set(least).at[spots[1]].set(largest)


def steps_of(rng, extent, cuts, low, largest):
    def one(position, parts):
        draws = jax.random.uniform(jax.random.fold_in(jax.random.fold_in(rng, 6), position), (parts,), jnp.float32, low / len(cuts), largest / len(cuts))
        return jnp.repeat(jnp.exp(draws), extent[position] // parts).reshape((-1,) + (1,) * (len(extent) - position - 1))

    gain = one(*cuts[0])
    for cut in cuts[1:]:
        gain = gain * one(*cut)
    return gain


def scatter_about(rng, extent, scale, most, pieces=(), kind=jnp.bfloat16):
    entries = jax.random.normal(rng, extent, jnp.float32) * scale
    if len(pieces) > 0:
        entries = steps_of(rng, extent, pieces, -0.22, 0.18) * entries
    return jnp.clip(entries, min=-most, max=most).astype(kind)


def setup_inputs(seed: int = 0) -> dict:
    arg_keys = jax.random.split(jax.random.key(seed), 9)
    thermal_anomaly = scatter_about(arg_keys[0], (DEPTH_LAYERS, PARALLEL_NUMBER, MERIDIAN_NUMBER), 1.0, 6.0, ((1, 16), (2, 32)), jnp.float32)
    saltiness_anomaly = scatter_about(arg_keys[1], (DEPTH_LAYERS, PARALLEL_NUMBER, MERIDIAN_NUMBER), 1.0, 6.0, ((1, 16), (2, 32)), jnp.float32)
    zonal_volume_flux = jnp.clip(jax.random.uniform(arg_keys[2], (DEPTH_LAYERS, PARALLEL_NUMBER, MERIDIAN_NUMBER), jnp.float32, -0.2, 0.2) * steps_of(arg_keys[2], (DEPTH_LAYERS, PARALLEL_NUMBER, MERIDIAN_NUMBER), ((1, 16), (2, 32)), -0.4, 0.0), -0.2, 0.2)
    meridional_volume_flux = jnp.clip(jax.random.uniform(arg_keys[3], (DEPTH_LAYERS, PARALLEL_NUMBER, MERIDIAN_NUMBER), jnp.float32, -0.2, 0.2) * steps_of(arg_keys[3], (DEPTH_LAYERS, PARALLEL_NUMBER, MERIDIAN_NUMBER), ((1, 16), (2, 32)), -0.4, 0.0), -0.2, 0.2)
    vertical_diffusion_factor = jnp.clip(jnp.exp(math.log(5.0) - 4.6051702 * jax.random.uniform(arg_keys[4], (DEPTH_LAYERS, PARALLEL_NUMBER, MERIDIAN_NUMBER), jnp.float32) ** steps_of(arg_keys[4], (DEPTH_LAYERS, PARALLEL_NUMBER, MERIDIAN_NUMBER), ((1, 16), (2, 32)), -0.2, 0.2)), 0.05, 5.0)
    friction_factor = jnp.clip(jnp.exp(math.log(3.0) - 3.4011974 * jax.random.uniform(arg_keys[5], (DEPTH_LAYERS, PARALLEL_NUMBER, MERIDIAN_NUMBER), jnp.float32) ** steps_of(arg_keys[5], (DEPTH_LAYERS, PARALLEL_NUMBER, MERIDIAN_NUMBER), ((1, 16), (2, 32)), -0.2, 0.2)), 0.1, 3.0)
    seawater_indicator = plant((jax.random.randint(arg_keys[6], (PARALLEL_NUMBER, MERIDIAN_NUMBER), 0, 5) < 4).astype(jnp.int32), jax.random.fold_in(arg_keys[6], 1), 0, 1)
    water_layer_depth = plant(jax.random.randint(arg_keys[7], (PARALLEL_NUMBER, MERIDIAN_NUMBER), 1, DEPTH_LAYERS + 1), jax.random.fold_in(arg_keys[7], 1), 1, DEPTH_LAYERS).astype(jnp.int32)
    return dict(thermal_anomaly=thermal_anomaly, saltiness_anomaly=saltiness_anomaly, zonal_volume_flux=zonal_volume_flux, meridional_volume_flux=meridional_volume_flux, vertical_diffusion_factor=vertical_diffusion_factor, friction_factor=friction_factor, seawater_indicator=seawater_indicator, water_layer_depth=water_layer_depth)


DIFFUSE = 0.05


def shifted_scalar(stacked):
    west_side = jnp.roll(stacked, 1, axis=-1)
    east_side = jnp.roll(stacked, -1, axis=-1)
    south_side = jnp.concatenate([jnp.zeros_like(stacked[..., :1, :]), stacked[..., :-1, :]], axis=-2)
    north_side = jnp.concatenate([stacked[..., 1:, :], stacked[..., -1:, ::-1]], axis=-2)
    return west_side, east_side, south_side, north_side


def tridiagonal(lower_band, main_band, upper_band, right_side):
    water_layer_number = main_band.shape[0]
    sweep_ratio = upper_band[0] / main_band[0]
    sweep_value = right_side[:, 0] / main_band[0]
    ratio_list = [sweep_ratio]
    value_list = [sweep_value]
    for level_index in range(1, water_layer_number):
        pivot_value = main_band[level_index] - lower_band[level_index] * sweep_ratio
        sweep_ratio = upper_band[level_index] / pivot_value
        sweep_value = (right_side[:, level_index] - lower_band[level_index] * sweep_value) / pivot_value
        ratio_list.append(sweep_ratio)
        value_list.append(sweep_value)
    solved_level = value_list[-1]
    solved_rows = [solved_level]
    for level_index in range(water_layer_number - 2, -1, -1):
        solved_level = value_list[level_index] - ratio_list[level_index] * solved_level
        solved_rows.append(solved_level)
    return jnp.stack(solved_rows[::-1], axis=1)


def march_scalars(thermal_anomaly, saltiness_anomaly, zonal_volume_flux, meridional_volume_flux, vertical_diffusion_factor, friction_factor, seawater_indicator, water_layer_depth, neighbour_sites, hinge_parallels, advection_passes):
    water_layer_number = thermal_anomaly.shape[0]
    depth_index = jnp.arange(water_layer_number, dtype=jnp.int32)[:, None, None]
    seawater_sites = jnp.where((seawater_indicator[None] == 1) & (depth_index < water_layer_depth[None]), 1.0, 0.0).astype(jnp.float32)
    damping = 1.0 + friction_factor
    east_flow = zonal_volume_flux / damping
    north_flow = meridional_volume_flux / damping
    west_side, east_side, south_side, north_side = neighbour_sites(jnp.stack([east_flow, north_flow, seawater_sites]))
    open_east = seawater_sites * east_side[2]
    open_west = west_side[2] * seawater_sites
    open_north = seawater_sites * north_side[2]
    open_south = south_side[2] * seawater_sites
    flow_west_face = west_side[0]
    flow_south_face = south_side[1]
    flow_north_face = jnp.where(hinge_parallels, 0.5 * (north_flow - north_side[1]), north_flow)
    scalar_quantities = jnp.stack([thermal_anomaly, saltiness_anomaly]) * seawater_sites
    for substep in range(advection_passes):
        west_tr, east_tr, south_tr, north_tr = neighbour_sites(scalar_quantities)
        flux_east = open_east * (jnp.maximum(east_flow, 0.0) * scalar_quantities + jnp.minimum(east_flow, 0.0) * east_tr - DIFFUSE * (east_tr - scalar_quantities))
        flux_west = open_west * (jnp.maximum(flow_west_face, 0.0) * west_tr + jnp.minimum(flow_west_face, 0.0) * scalar_quantities - DIFFUSE * (scalar_quantities - west_tr))
        flux_north = open_north * (jnp.maximum(flow_north_face, 0.0) * scalar_quantities + jnp.minimum(flow_north_face, 0.0) * north_tr - DIFFUSE * (north_tr - scalar_quantities))
        flux_south = open_south * (jnp.maximum(flow_south_face, 0.0) * south_tr + jnp.minimum(flow_south_face, 0.0) * scalar_quantities - DIFFUSE * (scalar_quantities - south_tr))
        scalar_quantities = scalar_quantities - (flux_east - flux_west + flux_north - flux_south)
    divergence = open_east * east_flow - open_west * flow_west_face + open_north * flow_north_face - open_south * flow_south_face
    deeper_sum = jnp.cumsum(divergence[::-1], axis=0)[::-1]
    zero_face = jnp.zeros_like(deeper_sum[:1])
    transport = -float(advection_passes) * jnp.concatenate([zero_face, deeper_sum[1:], zero_face], axis=0)
    mixing_faces = jnp.concatenate([zero_face, vertical_diffusion_factor[:-1] * seawater_sites[:-1] * seawater_sites[1:], zero_face], axis=0)
    main_band = 1.0 - jnp.minimum(transport[1:], 0.0) + mixing_faces[1:] + jnp.maximum(transport[:-1], 0.0) + mixing_faces[:-1]
    upper_band = -(jnp.maximum(transport[1:], 0.0) + mixing_faces[1:])
    lower_band = jnp.minimum(transport[:-1], 0.0) - mixing_faces[:-1]
    solved = tridiagonal(lower_band, main_band, upper_band, scalar_quantities)
    return solved[0], solved[1]


def reference(thermal_anomaly, saltiness_anomaly, zonal_volume_flux, meridional_volume_flux, vertical_diffusion_factor, friction_factor, seawater_indicator, water_layer_depth):
    parallel_number = thermal_anomaly.shape[1]
    hinge_parallels = (jnp.arange(parallel_number) == parallel_number - 1)[None, :, None]
    return march_scalars(thermal_anomaly, saltiness_anomaly, zonal_volume_flux, meridional_volume_flux, vertical_diffusion_factor, friction_factor, seawater_indicator, water_layer_depth, shifted_scalar, hinge_parallels, SPLIT_PASSES)
```

```python
import functools

import jax
import jax.numpy as jnp
from jax import lax
from jax.experimental import pallas as pl
from jax.experimental.pallas import tpu as pltpu
from jax.sharding import PartitionSpec as P

SPLIT_PASSES = 4
DIFFUSE = 0.05
TILE = (8, 128)
SPAN = 16
WINDOW = 8


def iotas():
    return (
        lax.broadcasted_iota(jnp.int32, TILE, 0),
        lax.broadcasted_iota(jnp.int32, TILE, 1),
    )


def roll(cells, shift, axis):
    return pltpu.roll(cells, shift, axis)


def flip_rows(cells, row):
    for bit in (1, 2, 4):
        cells = jnp.where((row & bit) != 0, roll(cells, bit, 0), roll(cells, 8 - bit, 0))
    return cells


def flip(cells, row, lanes):
    return flip_rows(jnp.take_along_axis(cells, lanes, axis=1), row)


def prep_kernel(
    flags, thermal, salty, zonal, meridional, friction, indicator, depth,
    east_out, north_out, first_out, second_out, count_out, pack_out,
):
    levels = thermal.shape[0]
    groups = -(-levels // SPAN)
    row, lane = iotas()
    natural = (row >> 2) == flags[0]
    count = jnp.where(indicator[...] == 1, depth[...], 0).astype(jnp.float32)
    count_out[...] = count
    first_out[2 * levels] = count
    second_out[2 * levels] = count

    def pack_level(m, packs):
        window = (lane >> 3) == m
        shift = 8 * m + 4
        packs = list(packs)
        for g in range(groups):
            k = jnp.minimum(SPAN * g + m, levels - 1)
            t, s = thermal[k], salty[k]
            ease = 1.0 / (1.0 + friction[k])
            e, n = zonal[k] * ease, meridional[k] * ease
            east_out[k] = e
            north_out[k] = n
            s4, n4 = roll(s, 4, 0), roll(n, 4, 0)
            first_out[2 * k] = jnp.where(natural, t, s4)
            second_out[2 * k] = jnp.where(natural, s4, t)
            first_out[2 * k + 1] = jnp.where(natural, e, n4)
            second_out[2 * k + 1] = jnp.where(natural, n4, e)
            for f, cells in enumerate((t, s, e, n)):
                spot = f * groups + g
                packs[spot] = jnp.where(window, roll(cells, shift, 1), packs[spot])
        packs[-1] = jnp.where(window, roll(count, shift, 1), packs[-1])
        return tuple(packs)

    blank = jnp.zeros(TILE, jnp.float32)
    packs = lax.fori_loop(0, SPAN, pack_level, (blank,) * (4 * groups + 1))
    for spot, cells in enumerate(packs):
        pack_out[spot] = cells

    @pl.when(flags[1] == 1)
    def _():
        lanes = 127 - lane
        first_out[2 * levels] = flip(count, row, lanes)

        def fold_level(k, carry):
            t, s = flip(thermal[k], row, lanes), flip(salty[k], row, lanes)
            e, n = -flip(east_out[k], row, lanes), -flip(north_out[k], row, lanes)
            first_out[2 * k] = jnp.where(row < 4, t, roll(s, 4, 0))
            first_out[2 * k + 1] = jnp.where(row < 4, e, roll(n, 4, 0))
            return carry

        lax.fori_loop(0, levels, fold_level, 0)


def corner_kernel(groups, flags, pack, from_west, from_east, first_out, second_out):
    row, lane = iotas()
    natural = (row >> 2) == flags[0]
    low = (lane & 7) < 4
    for spot in range(pack.shape[0]):
        own = pack[spot]
        left = jnp.where(low, from_west[spot], own)
        right = jnp.where(low, own, from_east[spot])
        right4 = roll(right, 4, 0)
        first_out[spot] = jnp.where(natural, left, right4)
        second_out[spot] = jnp.where(natural, right4, left)

    @pl.when(flags[1] == 1)
    def _():
        lanes = lane ^ 7
        for spot in range(pack.shape[0]):
            own = pack[spot]
            left = flip(jnp.where(low, from_west[spot], own), row, lanes)
            right = flip(jnp.where(low, own, from_east[spot]), row, lanes)
            if 2 * groups <= spot < 4 * groups:
                left, right = -left, -right
            first_out[spot] = jnp.where(row < 4, right, roll(left, 4, 0))


def northward(m, g, row):
    m, g = roll(m, 7, 0), roll(g, 7, 0)
    return jnp.where(row == 7, g, m), jnp.where(row == 7, m, g)


def southward(m, g, row):
    m, g = roll(m, 1, 0), roll(g, 1, 0)
    return jnp.where(row == 0, g, m), jnp.where(row == 0, m, g)


def coefficients(east, west, north, south, limits, level):
    open_east, open_west, open_north, open_south = (level < limit for limit in limits)
    leave_east = jnp.where(open_east, DIFFUSE + jnp.maximum(east, 0.0), 0.0)
    from_east = jnp.where(open_east, DIFFUSE - jnp.minimum(east, 0.0), 0.0)
    from_west = jnp.where(open_west, DIFFUSE + jnp.maximum(west, 0.0), 0.0)
    leave_west = jnp.where(open_west, DIFFUSE - jnp.minimum(west, 0.0), 0.0)
    leave_north = jnp.where(open_north, DIFFUSE + jnp.maximum(north, 0.0), 0.0)
    from_north = jnp.where(open_north, DIFFUSE - jnp.minimum(north, 0.0), 0.0)
    from_south = jnp.where(open_south, DIFFUSE + jnp.maximum(south, 0.0), 0.0)
    leave_south = jnp.where(open_south, DIFFUSE - jnp.minimum(south, 0.0), 0.0)
    stay = 1.0 - ((leave_east + leave_west) + (leave_north + leave_south))
    return stay, from_east, from_west, from_north, from_south


def apply(c, east, west, north, south, terms):
    stay, from_east, from_west, from_north, from_south = terms
    return (stay * c + (from_east * east + from_west * west)) + (
        from_north * north + from_south * south
    )


def step_kernel(
    flags, thermal, salty, east_in, north_in, mixing, count_in,
    first, second, pack, from_west, from_east, corner_first, corner_second,
    thermal_out, salty_out,
    feed, flow_feed, ratio,
):
    levels = thermal.shape[0]
    groups = -(-levels // SPAN)
    row, lane = iotas()
    natural = (row >> 2) == flags[0]
    top = flags[1] == 1
    top_row = (row == 7) & (flags[1] == 1)
    top_ghost = (row < 4) & (flags[1] == 1)
    low = (lane & 7) < 4
    at_west = (lane & 7) == 3

    def ghost_pair(a, b):
        return (
            jnp.where(natural, b, a),
            roll(jnp.where(natural, a, b), 4, 0),
        )

    def faces_north(n_m, n_g, row=row):
        n_up = roll(n_g, 7, 0)
        return (
            jnp.where(top_row, 0.5 * (n_m + n_up), n_m),
            jnp.where(top_ghost, n_up, n_g),
        )

    def merged(left, right):
        return jnp.where(at_west, left, roll(right, 126, 1))

    def sides(spot):
        own = pack[spot]
        left_m = jnp.where(low, from_west[spot], own)
        right_m = jnp.where(low, own, from_east[spot])
        left_g, right_g = ghost_pair(corner_first[spot], corner_second[spot])
        return (left_m, left_g), (right_m, right_g)

    counts = sides(4 * groups)
    count_feed = [merged(counts[0][i], counts[1][i]) for i in range(2)]
    for g in range(groups):
        level = (SPAN * g + (lane >> 3)).astype(jnp.float32)
        fields = [sides(f * groups + g) for f in range(4)]
        states = []
        edges = []
        for side in range(2):
            (t_m, t_g), (s_m, s_g), (e_m, e_g), (n_m, n_g) = (field[side] for field in fields)
            c_m, c_g = counts[side]
            up = northward(c_m, c_g, row)
            down = southward(c_m, c_g, row)
            raw_g = e_g
            e_g = jnp.where(top_ghost, roll(e_g, 127, 1), e_g)
            face_n = faces_north(n_m, n_g)
            face_s = southward(face_n[0], face_n[1], row)
            terms = []
            for i, (c, e) in enumerate(((c_m, e_m), (c_g, e_g))):
                limits = (
                    jnp.minimum(c, roll(c, 127, 1)),
                    jnp.minimum(c, roll(c, 1, 1)),
                    jnp.minimum(c, up[i]),
                    jnp.minimum(c, down[i]),
                )
                terms.append(
                    coefficients(e, roll(e, 1, 1), face_n[i], face_s[i], limits, level)
                )
            edges.append((e_m, e_g, raw_g))
            line = []
            for pair in ((t_m, t_g), (s_m, s_g)):
                pair = [
                    jnp.where(level < c, cells, 0.0) for cells, c in zip(pair, (c_m, c_g))
                ]
                track = [pair]
                for _ in range(SPLIT_PASSES - 1):
                    above = northward(pair[0], pair[1], row)
                    below = southward(pair[0], pair[1], row)
                    pair = [
                        apply(c, roll(c, 127, 1), roll(c, 1, 1), above[i], below[i], terms[i])
                        for i, c in enumerate(pair)
                    ]
                    track.append(pair)
                line.append(track)
            states.append(line)
        flow_feed[g] = merged(edges[0][0], edges[1][0])
        flow_feed[groups + g] = merged(edges[0][1], edges[1][2])
        for step in range(SPLIT_PASSES):
            for f in range(2):
                for i in range(2):
                    feed[((step * 2 + f) * 2 + i) * groups + g] = merged(
                        states[0][f][step][i], states[1][f][step][i]
                    )

    first_lane = lane == 0
    last_lane = lane == 127

    def eastward(c, beside):
        return jnp.where(last_lane, beside, roll(c, 127, 1))

    def westward(c, beside):
        return jnp.where(first_lane, beside, roll(c, 1, 1))

    count = (
        count_in[...],
        jnp.where(natural, second[2 * levels], first[2 * levels]),
    )
    count_beside = [roll(cells, 125, 1) for cells in count_feed]
    up = northward(count[0], count[1], row)
    down = southward(count[0], count[1], row)
    limits = [
        (
            jnp.minimum(count[i], eastward(count[i], count_beside[i])),
            jnp.minimum(count[i], westward(count[i], count_beside[i])),
            jnp.minimum(count[i], up[i]),
            jnp.minimum(count[i], down[i]),
        )
        for i in range(2)
    ]

    def level_step(index, carry):
        total, gain_up, gain_down, share, value_t, value_s = carry
        k = levels - 1 - index
        g = k >> 4
        shift = (125 - 8 * (k & 15)) & 127
        level = k.astype(jnp.float32)
        t_g, s_g = ghost_pair(first[2 * k], second[2 * k])
        e_g, n_g = ghost_pair(first[2 * k + 1], second[2 * k + 1])
        e_m, n_m = east_in[k], north_in[k]
        beside = [roll(flow_feed[i * groups + g], shift, 1) for i in range(2)]
        e_g = jnp.where(top_ghost, eastward(e_g, beside[1]), e_g)
        face_e = (e_m, e_g)
        face_w = [westward(face_e[i], beside[i]) for i in range(2)]
        face_n = faces_north(n_m, n_g)
        face_s = southward(face_n[0], face_n[1], row)
        terms = [
            coefficients(face_e[i], face_w[i], face_n[i], face_s[i], limits[i], level)
            for i in range(2)
        ]
        results = []
        for f, pair in enumerate(((thermal[k], t_g), (salty[k], s_g))):
            pair = [jnp.where(level < c, cells, 0.0) for cells, c in zip(pair, count)]
            for step in range(SPLIT_PASSES):
                above = northward(pair[0], pair[1], row)
                below = southward(pair[0], pair[1], row)
                last = step == SPLIT_PASSES - 1
                moved = []
                for i, c in enumerate(pair):
                    if last and i == 1:
                        continue
                    near = roll(feed[((step * 2 + f) * 2 + i) * groups + g], shift, 1)
                    moved.append(
                        apply(c, eastward(c, near), westward(c, near), above[i], below[i], terms[i])
                    )
                pair = moved
            results.append(pair[0])

        open_e, open_w, open_n, open_s = (level < limit for limit in limits[0])
        total = total + (
            (jnp.where(open_e, face_e[0], 0.0) - jnp.where(open_w, face_w[0], 0.0))
            + (jnp.where(open_n, face_n[0], 0.0) - jnp.where(open_s, face_s[0], 0.0))
        )
        inner = k > 0
        transport = jnp.where(inner, -float(SPLIT_PASSES) * total, 0.0)
        spread = jnp.where(
            (level < count[0]) & inner, mixing[jnp.maximum(k - 1, 0)], 0.0
        )
        new_down = jnp.maximum(transport, 0.0) + spread
        new_up = spread - jnp.minimum(transport, 0.0)
        pivot = (1.0 + gain_up + new_down) - gain_down * share
        inverse = 1.0 / pivot
        share = new_up * inverse
        value_t = (results[0] + gain_down * value_t) * inverse
        value_s = (results[1] + gain_down * value_s) * inverse
        ratio[k] = share
        thermal_out[k] = value_t
        salty_out[k] = value_s
        return total, new_up, new_down, share, value_t, value_s

    blank = jnp.zeros(TILE, jnp.float32)
    lax.fori_loop(0, levels, level_step, (blank,) * 6)

    def descend(k, carry):
        t, s = carry
        part = ratio[k]
        t = thermal_out[k] + part * t
        s = salty_out[k] + part * s
        thermal_out[k] = t
        salty_out[k] = s
        return t, s

    lax.fori_loop(1, levels, descend, (thermal_out[0], salty_out[0]))


def call(kernel, shapes, scratch=()):
    inner = pl.BlockSpec(memory_space=pltpu.VMEM)

    def run(flags, *arrays):
        return pl.pallas_call(
            kernel,
            out_shape=tuple(jax.ShapeDtypeStruct(shape, jnp.float32) for shape in shapes),
            in_specs=[pl.BlockSpec(memory_space=pltpu.SMEM)] + [inner] * len(arrays),
            out_specs=tuple(inner for _ in shapes),
            scratch_shapes=[pltpu.VMEM(shape, jnp.float32) for shape in scratch],
            compiler_params=pltpu.CompilerParams(vmem_limit_bytes=48 << 20),
        )(flags, *arrays)

    return run


def routes(lat_count, lon_count):
    first, second = [], []
    for lat in range(lat_count):
        even = (lat_count - 1 - lat) % 2 == 0
        for lon in range(lon_count):
            here = lon * lat_count + lat
            if lat == lat_count - 1:
                up = (lon_count - 1 - lon) * lat_count + lat
            else:
                up = here + 1
            down = here - 1
            (first if even else second).append((here, up))
            if lat > 0:
                (second if even else first).append((here, down))
    return first, second


def shards(
    thermal_anomaly,
    saltiness_anomaly,
    zonal_volume_flux,
    meridional_volume_flux,
    vertical_diffusion_factor,
    friction_factor,
    seawater_indicator,
    water_layer_depth,
):
    lat_count, lon_count = lax.axis_size("lat"), lax.axis_size("lon")
    lat = lax.axis_index("lat")
    levels = thermal_anomaly.shape[0]
    groups = -(-levels // SPAN)
    above = lat_count - 1 - lat
    flags = jnp.stack([1 - above % 2, (above == 0).astype(jnp.int32)]).astype(jnp.int32)
    field = (levels,) + TILE
    message = (2 * levels + 1,) + TILE
    packed = (4 * groups + 1,) + TILE

    east, north, first, second, count, pack = call(
        prep_kernel, (field, field, message, message, TILE, packed)
    )(
        flags, thermal_anomaly, saltiness_anomaly, zonal_volume_flux, meridional_volume_flux,
        friction_factor, seawater_indicator, water_layer_depth,
    )
    first_route, second_route = routes(lat_count, lon_count)
    both = ("lon", "lat")
    ring = [(i, (i + 1) % lon_count) for i in range(lon_count)]
    from_west = lax.ppermute(pack, "lon", ring)
    from_east = lax.ppermute(pack, "lon", [(b, a) for a, b in ring])
    first = lax.ppermute(first, both, first_route)
    second = lax.ppermute(second, both, second_route)
    corner_first, corner_second = call(
        functools.partial(corner_kernel, groups), (packed, packed)
    )(flags, pack, from_west, from_east)
    corner_first = lax.ppermute(corner_first, both, first_route)
    corner_second = lax.ppermute(corner_second, both, second_route)
    return call(
        step_kernel,
        (field, field),
        ((16 * groups,) + TILE, (2 * groups,) + TILE, field),
    )(
        flags, thermal_anomaly, saltiness_anomaly, east, north, vertical_diffusion_factor, count,
        first, second, pack, from_west, from_east, corner_first, corner_second,
    )


def solution(mesh):
    cells = P(None, "lat", "lon")
    columns = P("lat", "lon")
    return jax.shard_map(
        shards,
        mesh=mesh,
        in_specs=(cells,) * 6 + (columns,) * 2,
        out_specs=(cells, cells),
        check_vma=False,
    )
```

```python
import functools

import jax
import jax.numpy as jnp
from jax import lax
from jax.experimental import pallas as pl
from jax.experimental.pallas import tpu as pltpu
from jax.sharding import PartitionSpec as P

SPLIT_PASSES = 4
DIFFUSE = 0.05
TILE = (8, 128)
SPAN = 16
BATCH = 2


def iotas():
    return (
        lax.broadcasted_iota(jnp.int32, TILE, 0),
        lax.broadcasted_iota(jnp.int32, TILE, 1),
    )


def roll(cells, shift, axis):
    return pltpu.roll(cells, shift, axis)


def flip_rows(cells, row):
    for bit in (1, 2, 4):
        cells = jnp.where((row & bit) != 0, roll(cells, bit, 0), roll(cells, 8 - bit, 0))
    return cells


def flip(cells, row, lanes):
    return flip_rows(jnp.take_along_axis(cells, lanes, axis=1), row)


def pack_kernel(
    thermal, salty, zonal, meridional, friction, indicator, depth,
    east_out, north_out, count_out, pack_out,
    held, columns, arrived,
):
    levels = thermal.shape[0]
    groups = -(-levels // SPAN)
    row, lane = iotas()
    flat = [
        pltpu.make_async_copy(source, columns.at[i], arrived.at[groups, i])
        for i, source in enumerate((indicator, depth))
    ]
    for copy in flat:
        copy.start()
    sources = (thermal, salty, zonal, meridional, friction)
    copies = []
    for g in range(groups):
        part = pl.ds(SPAN * g, min(SPAN, levels - SPAN * g))
        copies.append(
            [
                pltpu.make_async_copy(
                    source.at[part], held.at[f, part], arrived.at[g, f]
                )
                for f, source in enumerate(sources)
            ]
        )
        for copy in copies[-1]:
            copy.start()
    for copy in flat:
        copy.wait()
    count = jnp.where(columns[0] == 1, columns[1], 0).astype(jnp.float32)
    count_out[...] = count
    spread = count
    for m in range(SPAN):
        spread = jnp.where((lane >> 3) == m, roll(count, 8 * m + 4, 1), spread)
    pack_out[4 * groups] = spread

    for g in range(groups):
        for copy in copies[g]:
            copy.wait()

        def pack_levels(index, packs, g=g):
            packs = list(packs)
            for u in range(2):
                m = 2 * index + u
                k = SPAN * g + m
                window = (lane >> 3) == m
                ease = 1.0 / (1.0 + held[4, k])
                e, n = held[2, k] * ease, held[3, k] * ease
                east_out[k] = e
                north_out[k] = n
                for f, cells in enumerate((held[0, k], held[1, k], e, n)):
                    packs[f] = jnp.where(window, roll(cells, 8 * m + 4, 1), packs[f])
            return tuple(packs)

        depth_here = min(SPAN, levels - SPAN * g)
        blank = jnp.zeros(TILE, jnp.float32)
        packs = lax.fori_loop(0, depth_here // 2, pack_levels, (blank,) * 4)
        for f in range(4):
            pack_out[f * groups + g] = packs[f]


def bulk_kernel(flags, thermal, salty, east, north, count, first_out, second_out):
    levels = thermal.shape[0]
    row, lane = iotas()
    natural = (row >> 2) == flags[0]
    first_out[2 * levels] = count[...]
    second_out[2 * levels] = count[...]

    def levels_of(index, carry):
        for u in range(2):
            k = 2 * index + u
            t, e = thermal[k], east[k]
            s4, n4 = roll(salty[k], 4, 0), roll(north[k], 4, 0)
            first_out[2 * k] = jnp.where(natural, t, s4)
            second_out[2 * k] = jnp.where(natural, s4, t)
            first_out[2 * k + 1] = jnp.where(natural, e, n4)
            second_out[2 * k + 1] = jnp.where(natural, n4, e)
        return carry

    lax.fori_loop(0, levels // 2, levels_of, 0)

    @pl.when(flags[1] == 1)
    def _():
        lanes = 127 - lane
        first_out[2 * levels] = flip(count[...], row, lanes)

        def fold_levels(index, carry):
            tiles = []
            for u in range(4):
                j = 4 * index + u
                tile = flip(first_out[j], row, lanes)
                tiles.append(-tile if u % 2 == 1 else tile)
            for u in range(4):
                first_out[4 * index + u] = tiles[u]
            return carry

        lax.fori_loop(0, levels // 2, fold_levels, 0)


def corner_kernel(
    groups, flags, first_in, second_in, pack, from_west, from_east,
    first_out, second_out,
    held, arrived,
):
    del first_in, second_in
    row, lane = iotas()
    natural = (row >> 2) == flags[0]
    low = (lane & 7) < 4
    size = pack.shape[0]
    for spot in range(size):
        own = pack[spot]
        left = jnp.where(low, from_west[spot], own)
        right = jnp.where(low, own, from_east[spot])
        right4 = roll(right, 4, 0)
        held[0, spot] = jnp.where(natural, left, right4)
        held[1, spot] = jnp.where(natural, right4, left)

    @pl.when(flags[1] == 1)
    def _():
        lanes = lane ^ 7
        tiles = []
        for spot in range(size):
            own = pack[spot]
            left = jnp.where(low, from_west[spot], own)
            right = jnp.where(low, own, from_east[spot])
            tile = flip(jnp.where(row < 4, roll(left, 4, 0), right), row, lanes)
            tiles.append(-tile if 2 * groups <= spot < 4 * groups else tile)
        for spot, tile in enumerate(tiles):
            held[0, spot] = tile

    copies = []
    for i, target in enumerate((first_out, second_out)):
        part = pl.ds(target.shape[0] - size, size)
        copies.append(pltpu.make_async_copy(held.at[i], target.at[part], arrived.at[i]))
    for copy in copies:
        copy.start()
    for copy in copies:
        copy.wait()


def northward(m, g, row):
    m, g = roll(m, 7, 0), roll(g, 7, 0)
    return jnp.where(row == 7, g, m), jnp.where(row == 7, m, g)


def southward(m, g, row):
    m, g = roll(m, 1, 0), roll(g, 1, 0)
    return jnp.where(row == 0, g, m), jnp.where(row == 0, m, g)


def coefficients(east, west, north, south, limits, level):
    open_east, open_west, open_north, open_south = (level < limit for limit in limits)
    leave_east = jnp.where(open_east, DIFFUSE + jnp.maximum(east, 0.0), 0.0)
    from_east = jnp.where(open_east, DIFFUSE - jnp.minimum(east, 0.0), 0.0)
    from_west = jnp.where(open_west, DIFFUSE + jnp.maximum(west, 0.0), 0.0)
    leave_west = jnp.where(open_west, DIFFUSE - jnp.minimum(west, 0.0), 0.0)
    leave_north = jnp.where(open_north, DIFFUSE + jnp.maximum(north, 0.0), 0.0)
    from_north = jnp.where(open_north, DIFFUSE - jnp.minimum(north, 0.0), 0.0)
    from_south = jnp.where(open_south, DIFFUSE + jnp.maximum(south, 0.0), 0.0)
    leave_south = jnp.where(open_south, DIFFUSE - jnp.minimum(south, 0.0), 0.0)
    stay = 1.0 - ((leave_east + leave_west) + (leave_north + leave_south))
    return stay, from_east, from_west, from_north, from_south


def apply(c, east, west, north, south, terms):
    stay, from_east, from_west, from_north, from_south = terms
    return (stay * c + (from_east * east + from_west * west)) + (
        from_north * north + from_south * south
    )


def step_kernel(
    flags, thermal, salty, east_in, north_in, mixing, count_in,
    first, second, pack, from_west, from_east,
    thermal_out, salty_out,
    feed, flow_feed, ratio,
):
    levels = thermal.shape[0]
    groups = -(-levels // SPAN)
    row, lane = iotas()
    natural = (row >> 2) == flags[0]
    top_row = (row == 7) & (flags[1] == 1)
    top_ghost = (row < 4) & (flags[1] == 1)
    low = (lane & 7) < 4
    at_west = (lane & 7) == 3

    def ghost_pair(a, b):
        return (
            jnp.where(natural, b, a),
            roll(jnp.where(natural, a, b), 4, 0),
        )

    def faces_north(n_m, n_g):
        n_up = roll(n_g, 7, 0)
        return (
            jnp.where(top_row, 0.5 * (n_m + n_up), n_m),
            jnp.where(top_ghost, n_up, n_g),
        )

    def merged(left, right):
        return jnp.where(at_west, left, roll(right, 126, 1))

    base = 2 * levels + 1

    def sides(spot):
        own = pack[spot]
        left_m = jnp.where(low, from_west[spot], own)
        right_m = jnp.where(low, own, from_east[spot])
        left_g, right_g = ghost_pair(first[base + spot], second[base + spot])
        return (left_m, left_g), (right_m, right_g)

    counts = sides(4 * groups)
    count_feed = [merged(counts[0][i], counts[1][i]) for i in range(2)]
    for g in range(groups):
        level = (SPAN * g + (lane >> 3)).astype(jnp.float32)
        fields = [sides(f * groups + g) for f in range(4)]
        states = []
        edges = []
        for side in range(2):
            (t_m, t_g), (s_m, s_g), (e_m, e_g), (n_m, n_g) = (field[side] for field in fields)
            c_m, c_g = counts[side]
            up = northward(c_m, c_g, row)
            down = southward(c_m, c_g, row)
            raw_g = e_g
            e_g = jnp.where(top_ghost, roll(e_g, 127, 1), e_g)
            face_n = faces_north(n_m, n_g)
            face_s = southward(face_n[0], face_n[1], row)
            terms = []
            for i, (c, e) in enumerate(((c_m, e_m), (c_g, e_g))):
                limits = (
                    jnp.minimum(c, roll(c, 127, 1)),
                    jnp.minimum(c, roll(c, 1, 1)),
                    jnp.minimum(c, up[i]),
                    jnp.minimum(c, down[i]),
                )
                terms.append(
                    coefficients(e, roll(e, 1, 1), face_n[i], face_s[i], limits, level)
                )
            edges.append((e_m, e_g, raw_g))
            line = []
            for pair in ((t_m, t_g), (s_m, s_g)):
                pair = [
                    jnp.where(level < c, cells, 0.0) for cells, c in zip(pair, (c_m, c_g))
                ]
                track = [pair]
                for _ in range(SPLIT_PASSES - 1):
                    above = northward(pair[0], pair[1], row)
                    below = southward(pair[0], pair[1], row)
                    pair = [
                        apply(c, roll(c, 127, 1), roll(c, 1, 1), above[i], below[i], terms[i])
                        for i, c in enumerate(pair)
                    ]
                    track.append(pair)
                line.append(track)
            states.append(line)
        flow_feed[g] = merged(edges[0][0], edges[1][0])
        flow_feed[groups + g] = merged(edges[0][1], edges[1][2])
        for step in range(SPLIT_PASSES):
            for f in range(2):
                for i in range(2):
                    feed[((step * 2 + f) * 2 + i) * groups + g] = merged(
                        states[0][f][step][i], states[1][f][step][i]
                    )

    first_lane = lane == 0
    last_lane = lane == 127

    def eastward(c, beside):
        return jnp.where(last_lane, beside, roll(c, 127, 1))

    def westward(c, beside):
        return jnp.where(first_lane, beside, roll(c, 1, 1))

    count = (
        count_in[...],
        jnp.where(natural, second[2 * levels], first[2 * levels]),
    )
    count_beside = [roll(cells, 125, 1) for cells in count_feed]
    up = northward(count[0], count[1], row)
    down = southward(count[0], count[1], row)
    limits = [
        (
            jnp.minimum(count[i], eastward(count[i], count_beside[i])),
            jnp.minimum(count[i], westward(count[i], count_beside[i])),
            jnp.minimum(count[i], up[i]),
            jnp.minimum(count[i], down[i]),
        )
        for i in range(2)
    ]

    def prepare(k):
        g = k >> 4
        shift = (125 - 8 * (k & 15)) & 127
        level = k.astype(jnp.float32)
        t_g, s_g = ghost_pair(first[2 * k], second[2 * k])
        e_g, n_g = ghost_pair(first[2 * k + 1], second[2 * k + 1])
        e_m, n_m = east_in[k], north_in[k]
        beside = [roll(flow_feed[i * groups + g], shift, 1) for i in range(2)]
        e_g = jnp.where(top_ghost, eastward(e_g, beside[1]), e_g)
        face_e = (e_m, e_g)
        face_w = [westward(face_e[i], beside[i]) for i in range(2)]
        face_n = faces_north(n_m, n_g)
        face_s = southward(face_n[0], face_n[1], row)
        terms = [
            coefficients(face_e[i], face_w[i], face_n[i], face_s[i], limits[i], level)
            for i in range(2)
        ]
        states = [
            [jnp.where(level < c, cells, 0.0) for cells, c in zip(pair, count)]
            for pair in ((thermal[k], t_g), (salty[k], s_g))
        ]
        open_e, open_w, open_n, open_s = (level < limit for limit in limits[0])
        outflow = (jnp.where(open_e, face_e[0], 0.0) - jnp.where(open_w, face_w[0], 0.0)) + (
            jnp.where(open_n, face_n[0], 0.0) - jnp.where(open_s, face_s[0], 0.0)
        )
        inner = k > 0
        spread = jnp.where(
            (level < count[0]) & inner, mixing[jnp.maximum(k - 1, 0)], 0.0
        )
        return g, shift, terms, states, outflow, inner, spread

    def advance(step, g, shift, terms, states):
        moved_states = []
        for f, pair in enumerate(states):
            above = northward(pair[0], pair[1], row)
            below = southward(pair[0], pair[1], row)
            moved = []
            for i, c in enumerate(pair):
                if step == SPLIT_PASSES - 1 and i == 1:
                    continue
                near = roll(feed[((step * 2 + f) * 2 + i) * groups + g], shift, 1)
                moved.append(
                    apply(c, eastward(c, near), westward(c, near), above[i], below[i], terms[i])
                )
            moved_states.append(moved)
        return moved_states

    def some_levels(bottom, number, carry):
        total, gain_up, gain_down, share, value_t, value_s = carry
        rows = [bottom - u for u in range(number)]
        ready = [prepare(k) for k in rows]
        states = [r[3] for r in ready]
        for step in range(SPLIT_PASSES):
            states = [advance(step, *r[:3], state) for r, state in zip(ready, states)]
        for k, r, state in zip(rows, ready, states):
            outflow, inner, spread = r[4:]
            total = total + outflow
            transport = jnp.where(inner, -float(SPLIT_PASSES) * total, 0.0)
            new_down = jnp.maximum(transport, 0.0) + spread
            new_up = spread - jnp.minimum(transport, 0.0)
            pivot = (1.0 + gain_up + new_down) - gain_down * share
            inverse = 1.0 / pivot
            share = new_up * inverse
            value_t = (state[0][0] + gain_down * value_t) * inverse
            value_s = (state[1][0] + gain_down * value_s) * inverse
            gain_up, gain_down = new_up, new_down
            ratio[k] = share
            thermal_out[k] = value_t
            salty_out[k] = value_s
        return total, gain_up, gain_down, share, value_t, value_s

    carry = (jnp.zeros(TILE, jnp.float32),) * 6
    whole, left = divmod(levels, BATCH)
    carry = lax.fori_loop(
        0, whole, lambda i, c: some_levels(levels - 1 - BATCH * i, BATCH, c), carry
    )
    if left:
        some_levels(jnp.int32(left - 1), left, carry)

    def descend(k, carry):
        t, s = carry
        part = ratio[k]
        t = thermal_out[k] + part * t
        s = salty_out[k] + part * s
        thermal_out[k] = t
        salty_out[k] = s
        return t, s

    lax.fori_loop(1, levels, descend, (thermal_out[0], salty_out[0]))


def call(kernel, shapes, scratch=(), flags=None, direct=0, place=pltpu.HBM, shared=False):
    inner = pl.BlockSpec(memory_space=pltpu.VMEM)
    outer = pl.BlockSpec(memory_space=place)

    def run(*arrays):
        specs = [outer] * direct + [inner] * (len(arrays) - direct)
        if flags is not None:
            arrays = (flags,) + arrays
            specs = [pl.BlockSpec(memory_space=pltpu.SMEM)] + specs
        return pl.pallas_call(
            kernel,
            out_shape=tuple(jax.ShapeDtypeStruct(shape, jnp.float32) for shape in shapes),
            in_specs=specs,
            out_specs=tuple(outer if shared else inner for _ in shapes),
            scratch_shapes=list(scratch),
            input_output_aliases={1: 0, 2: 1} if shared else {},
            compiler_params=pltpu.CompilerParams(vmem_limit_bytes=32 << 20),
        )(*arrays)

    return run


def routes(lat_count, lon_count):
    first, second = [], []
    for lat in range(lat_count):
        even = (lat_count - 1 - lat) % 2 == 0
        for lon in range(lon_count):
            here = lon * lat_count + lat
            if lat == lat_count - 1:
                up = (lon_count - 1 - lon) * lat_count + lat
            else:
                up = here + 1
            down = here - 1
            (first if even else second).append((here, up))
            if lat > 0:
                (second if even else first).append((here, down))
    return first, second


def shards(
    thermal_anomaly,
    saltiness_anomaly,
    zonal_volume_flux,
    meridional_volume_flux,
    vertical_diffusion_factor,
    friction_factor,
    seawater_indicator,
    water_layer_depth,
):
    lat_count, lon_count = lax.axis_size("lat"), lax.axis_size("lon")
    lat = lax.axis_index("lat")
    levels = thermal_anomaly.shape[0]
    groups = -(-levels // SPAN)
    above = lat_count - 1 - lat
    flags = jnp.stack([1 - above % 2, (above == 0).astype(jnp.int32)]).astype(jnp.int32)
    field = (levels,) + TILE
    packed = (4 * groups + 1,) + TILE
    message = (2 * levels + 1 + packed[0],) + TILE

    east, north, count, pack = call(
        pack_kernel,
        (field, field, TILE, packed),
        (
            pltpu.VMEM((5,) + field, jnp.float32),
            pltpu.VMEM((2,) + TILE, jnp.int32),
            pltpu.SemaphoreType.DMA((groups + 1, 5)),
        ),
        direct=7,
    )(
        *(
            pltpu.with_memory_space_constraint(field_in, pltpu.HBM)
            for field_in in (
                thermal_anomaly,
                saltiness_anomaly,
                zonal_volume_flux,
                meridional_volume_flux,
                friction_factor,
                seawater_indicator,
                water_layer_depth,
            )
        )
    )
    ring = [(i, (i + 1) % lon_count) for i in range(lon_count)]
    from_west = lax.ppermute(pack, "lon", ring)
    from_east = lax.ppermute(pack, "lon", [(b, a) for a, b in ring])
    first, second = call(bulk_kernel, (message, message), flags=flags)(
        thermal_anomaly, saltiness_anomaly, east, north, count
    )
    first, second = call(
        functools.partial(corner_kernel, groups),
        (message, message),
        (pltpu.VMEM((2,) + packed, jnp.float32), pltpu.SemaphoreType.DMA((2,))),
        flags=flags,
        direct=2,
        place=pl.ANY,
        shared=True,
    )(first, second, pack, from_west, from_east)
    first_route, second_route = routes(lat_count, lon_count)
    both = ("lon", "lat")
    first = lax.ppermute(first, both, first_route)
    second = lax.ppermute(second, both, second_route)
    return call(
        step_kernel,
        (field, field),
        (
            pltpu.VMEM((16 * groups,) + TILE, jnp.float32),
            pltpu.VMEM((2 * groups,) + TILE, jnp.float32),
            pltpu.VMEM(field, jnp.float32),
        ),
        flags=flags,
    )(
        thermal_anomaly, saltiness_anomaly, east, north, vertical_diffusion_factor, count,
        first, second, pack, from_west, from_east,
    )


def solution(mesh):
    cells = P(None, "lat", "lon")
    columns = P("lat", "lon")
    return jax.shard_map(
        shards,
        mesh=mesh,
        in_specs=(cells,) * 6 + (columns,) * 2,
        out_specs=(cells, cells),
        check_vma=False,
    )
```

```python
import functools

import jax
import jax.numpy as jnp
from jax import lax
from jax.experimental import pallas as pl
from jax.experimental.pallas import tpu as pltpu
from jax.sharding import PartitionSpec as P

SPLIT_PASSES = 4
DIFFUSE = 0.05
TILE = (8, 128)
SPAN = 16
BATCH = 10, 8


def iotas():
    return (
        lax.broadcasted_iota(jnp.int32, TILE, 0),
        lax.broadcasted_iota(jnp.int32, TILE, 1),
    )


def roll(cells, shift, axis):
    return pltpu.roll(cells, shift, axis)


def flip_rows(cells, row):
    for bit in (1, 2, 4):
        cells = jnp.where((row & bit) != 0, roll(cells, bit, 0), roll(cells, 8 - bit, 0))
    return cells


def flip(cells, row, lanes):
    return flip_rows(jnp.take_along_axis(cells, lanes, axis=1), row)


def shared_tiles(t, s, e, n, natural):
    s4, n4 = roll(s, 4, 0), roll(n, 4, 0)
    return (
        (jnp.where(natural, t, s4), jnp.where(natural, e, n4)),
        (jnp.where(natural, s4, t), jnp.where(natural, n4, e)),
    )


def fold_tiles(target, number, together, row, lane):
    lanes = 127 - lane

    def some_tiles(index, carry):
        tiles = [
            flip(target[together * index + u], row, lanes) for u in range(together)
        ]
        for u, tile in enumerate(tiles):
            target[together * index + u] = -tile if u % 2 == 1 else tile
        return carry

    lax.fori_loop(0, number // together, some_tiles, 0)


def pack_kernel(
    flags, thermal, salty, zonal, meridional, friction, indicator, depth,
    east_out, north_out, count_out, pack_out, first_out, second_out,
    held, columns, arrived,
):
    levels = thermal.shape[0]
    groups = -(-levels // SPAN)
    row, lane = iotas()
    natural = (row >> 2) == flags[0]
    flat = [
        pltpu.make_async_copy(source, columns.at[i], arrived.at[groups, i])
        for i, source in enumerate((indicator, depth))
    ]
    for copy in flat:
        copy.start()
    sources = (thermal, salty, zonal, meridional, friction)
    copies = {}
    for g in reversed(range(groups)):
        part = pl.ds(SPAN * g, min(SPAN, levels - SPAN * g))
        copies[g] = [
            pltpu.make_async_copy(source.at[part], held.at[f, part], arrived.at[g, f])
            for f, source in enumerate(sources)
        ]
        for copy in copies[g]:
            copy.start()
    for copy in flat:
        copy.wait()
    count = jnp.where(columns[0] == 1, columns[1], 0).astype(jnp.float32)
    count_out[...] = count
    top_spot = 2 * (levels - SPAN)
    first_out[top_spot] = count
    second_out[top_spot] = count
    spread = count
    for m in range(SPAN):
        spread = jnp.where((lane >> 3) == m, roll(count, 8 * m + 4, 1), spread)
    pack_out[4 * groups] = spread

    for g in reversed(range(groups)):
        here = min(SPAN, levels - SPAN * g)
        together = here // 2
        for copy in copies[g]:
            copy.wait()

        def pack_levels(index, packs, g=g, together=together):
            packs = list(packs)
            for u in range(together):
                m = together * index + u
                k = SPAN * g + m
                window = (lane >> 3) == m
                t, s = held[0, k], held[1, k]
                ease = 1.0 / (1.0 + held[4, k])
                e, n = held[2, k] * ease, held[3, k] * ease
                east_out[k] = e
                north_out[k] = n
                if g > 0:
                    spot = 2 * (k - SPAN)
                    firsts, seconds = shared_tiles(t, s, e, n, natural)
                    for i in range(2):
                        first_out[spot + i] = firsts[i]
                        second_out[spot + i] = seconds[i]
                for f, cells in enumerate((t, s, e, n)):
                    packs[f] = jnp.where(window, roll(cells, 8 * m + 4, 1), packs[f])
            return tuple(packs)

        blank = jnp.zeros(TILE, jnp.float32)
        packs = lax.fori_loop(0, 2, pack_levels, (blank,) * 4)
        for f in range(4):
            pack_out[f * groups + g] = packs[f]

    @pl.when(flags[1] == 1)
    def _():
        first_out[top_spot] = flip(count, row, 127 - lane)
        fold_tiles(first_out, top_spot, 12, row, lane)


def bulk_kernel(flags, thermal, salty, east, north, first_out, second_out):
    row, lane = iotas()
    natural = (row >> 2) == flags[0]

    def levels_of(index, carry):
        for u in range(SPAN // 2):
            k = SPAN // 2 * index + u
            firsts, seconds = shared_tiles(thermal[k], salty[k], east[k], north[k], natural)
            for i in range(2):
                first_out[2 * k + i] = firsts[i]
                second_out[2 * k + i] = seconds[i]
        return carry

    lax.fori_loop(0, 2, levels_of, 0)

    @pl.when(flags[1] == 1)
    def _():
        fold_tiles(first_out, 2 * SPAN, 16, row, lane)


def corner_kernel(
    groups, flags, first_in, second_in, pack, from_west, from_east,
    first_out, second_out,
    held, arrived,
):
    del first_in, second_in
    row, lane = iotas()
    natural = (row >> 2) == flags[0]
    low = (lane & 7) < 4
    size = pack.shape[0]
    for spot in range(size):
        own = pack[spot]
        left = jnp.where(low, from_west[spot], own)
        right = jnp.where(low, own, from_east[spot])
        right4 = roll(right, 4, 0)
        held[0, spot] = jnp.where(natural, left, right4)
        held[1, spot] = jnp.where(natural, right4, left)

    @pl.when(flags[1] == 1)
    def _():
        lanes = lane ^ 7
        tiles = []
        for spot in range(size):
            own = pack[spot]
            left = jnp.where(low, from_west[spot], own)
            right = jnp.where(low, own, from_east[spot])
            tile = flip(jnp.where(row < 4, roll(left, 4, 0), right), row, lanes)
            tiles.append(-tile if 2 * groups <= spot < 4 * groups else tile)
        for spot, tile in enumerate(tiles):
            held[0, spot] = tile

    copies = []
    for i, target in enumerate((first_out, second_out)):
        part = pl.ds(target.shape[0] - size, size)
        copies.append(pltpu.make_async_copy(held.at[i], target.at[part], arrived.at[i]))
    for copy in copies:
        copy.start()
    for copy in copies:
        copy.wait()


def northward(m, g, row):
    m, g = roll(m, 7, 0), roll(g, 7, 0)
    return jnp.where(row == 7, g, m), jnp.where(row == 7, m, g)


def southward(m, g, row):
    m, g = roll(m, 1, 0), roll(g, 1, 0)
    return jnp.where(row == 0, g, m), jnp.where(row == 0, m, g)


def coefficients(east, west, north, south, limits, level):
    open_east, open_west, open_north, open_south = (level < limit for limit in limits)
    leave_east = jnp.where(open_east, DIFFUSE + jnp.maximum(east, 0.0), 0.0)
    from_east = jnp.where(open_east, DIFFUSE - jnp.minimum(east, 0.0), 0.0)
    from_west = jnp.where(open_west, DIFFUSE + jnp.maximum(west, 0.0), 0.0)
    leave_west = jnp.where(open_west, DIFFUSE - jnp.minimum(west, 0.0), 0.0)
    leave_north = jnp.where(open_north, DIFFUSE + jnp.maximum(north, 0.0), 0.0)
    from_north = jnp.where(open_north, DIFFUSE - jnp.minimum(north, 0.0), 0.0)
    from_south = jnp.where(open_south, DIFFUSE + jnp.maximum(south, 0.0), 0.0)
    leave_south = jnp.where(open_south, DIFFUSE - jnp.minimum(south, 0.0), 0.0)
    stay = 1.0 - ((leave_east + leave_west) + (leave_north + leave_south))
    return stay, from_east, from_west, from_north, from_south


def apply(c, east, west, north, south, terms):
    stay, from_east, from_west, from_north, from_south = terms
    return (stay * c + (from_east * east + from_west * west)) + (
        from_north * north + from_south * south
    )


def step_kernel(
    flags, thermal, salty, east_in, north_in, mixing, count_in,
    first, second, first_top, second_top, pack, from_west, from_east,
    thermal_out, salty_out,
    feed, flow_feed, ratio,
):
    levels = thermal.shape[0]
    groups = -(-levels // SPAN)
    row, lane = iotas()
    natural = (row >> 2) == flags[0]
    top_row = (row == 7) & (flags[1] == 1)
    top_ghost = (row < 4) & (flags[1] == 1)
    low = (lane & 7) < 4
    at_west = (lane & 7) == 3

    def ghost_pair(a, b):
        return (
            jnp.where(natural, b, a),
            roll(jnp.where(natural, a, b), 4, 0),
        )

    def faces_north(n_m, n_g):
        n_up = roll(n_g, 7, 0)
        return (
            jnp.where(top_row, 0.5 * (n_m + n_up), n_m),
            jnp.where(top_ghost, n_up, n_g),
        )

    def merged(left, right):
        return jnp.where(at_west, left, roll(right, 126, 1))

    base = 2 * SPAN

    def sides(spot):
        own = pack[spot]
        left_m = jnp.where(low, from_west[spot], own)
        right_m = jnp.where(low, own, from_east[spot])
        left_g, right_g = ghost_pair(first_top[base + spot], second_top[base + spot])
        return (left_m, left_g), (right_m, right_g)

    counts = sides(4 * groups)
    count_feed = [merged(counts[0][i], counts[1][i]) for i in range(2)]
    for g in range(groups):
        level = (SPAN * g + (lane >> 3)).astype(jnp.float32)
        fields = [sides(f * groups + g) for f in range(4)]
        states = []
        edges = []
        for side in range(2):
            (t_m, t_g), (s_m, s_g), (e_m, e_g), (n_m, n_g) = (field[side] for field in fields)
            c_m, c_g = counts[side]
            up = northward(c_m, c_g, row)
            down = southward(c_m, c_g, row)
            raw_g = e_g
            e_g = jnp.where(top_ghost, roll(e_g, 127, 1), e_g)
            face_n = faces_north(n_m, n_g)
            face_s = southward(face_n[0], face_n[1], row)
            terms = []
            for i, (c, e) in enumerate(((c_m, e_m), (c_g, e_g))):
                limits = (
                    jnp.minimum(c, roll(c, 127, 1)),
                    jnp.minimum(c, roll(c, 1, 1)),
                    jnp.minimum(c, up[i]),
                    jnp.minimum(c, down[i]),
                )
                terms.append(
                    coefficients(e, roll(e, 1, 1), face_n[i], face_s[i], limits, level)
                )
            edges.append((e_m, e_g, raw_g))
            line = []
            for pair in ((t_m, t_g), (s_m, s_g)):
                pair = [
                    jnp.where(level < c, cells, 0.0) for cells, c in zip(pair, (c_m, c_g))
                ]
                track = [pair]
                for _ in range(SPLIT_PASSES - 1):
                    above = northward(pair[0], pair[1], row)
                    below = southward(pair[0], pair[1], row)
                    pair = [
                        apply(c, roll(c, 127, 1), roll(c, 1, 1), above[i], below[i], terms[i])
                        for i, c in enumerate(pair)
                    ]
                    track.append(pair)
                line.append(track)
            states.append(line)
        flow_feed[g] = merged(edges[0][0], edges[1][0])
        flow_feed[groups + g] = merged(edges[0][1], edges[1][2])
        for step in range(SPLIT_PASSES):
            for f in range(2):
                for i in range(2):
                    feed[((step * 2 + f) * 2 + i) * groups + g] = merged(
                        states[0][f][step][i], states[1][f][step][i]
                    )

    first_lane = lane == 0
    last_lane = lane == 127

    def eastward(c, beside):
        return jnp.where(last_lane, beside, roll(c, 127, 1))

    def westward(c, beside):
        return jnp.where(first_lane, beside, roll(c, 1, 1))

    count = (
        count_in[...],
        jnp.where(natural, second[2 * (levels - SPAN)], first[2 * (levels - SPAN)]),
    )
    count_beside = [roll(cells, 125, 1) for cells in count_feed]
    up = northward(count[0], count[1], row)
    down = southward(count[0], count[1], row)
    limits = [
        (
            jnp.minimum(count[i], eastward(count[i], count_beside[i])),
            jnp.minimum(count[i], westward(count[i], count_beside[i])),
            jnp.minimum(count[i], up[i]),
            jnp.minimum(count[i], down[i]),
        )
        for i in range(2)
    ]

    def prepare(k, ghosts, spot):
        g = k >> 4
        shift = (125 - 8 * (k & 15)) & 127
        level = k.astype(jnp.float32)
        t_g, s_g = ghost_pair(ghosts[0][spot], ghosts[1][spot])
        e_g, n_g = ghost_pair(ghosts[0][spot + 1], ghosts[1][spot + 1])
        e_m, n_m = east_in[k], north_in[k]
        beside = [roll(flow_feed[i * groups + g], shift, 1) for i in range(2)]
        e_g = jnp.where(top_ghost, eastward(e_g, beside[1]), e_g)
        face_e = (e_m, e_g)
        face_w = [westward(face_e[i], beside[i]) for i in range(2)]
        face_n = faces_north(n_m, n_g)
        face_s = southward(face_n[0], face_n[1], row)
        terms = [
            coefficients(face_e[i], face_w[i], face_n[i], face_s[i], limits[i], level)
            for i in range(2)
        ]
        states = [
            [jnp.where(level < c, cells, 0.0) for cells, c in zip(pair, count)]
            for pair in ((thermal[k], t_g), (salty[k], s_g))
        ]
        open_e, open_w, open_n, open_s = (level < limit for limit in limits[0])
        outflow = (jnp.where(open_e, face_e[0], 0.0) - jnp.where(open_w, face_w[0], 0.0)) + (
            jnp.where(open_n, face_n[0], 0.0) - jnp.where(open_s, face_s[0], 0.0)
        )
        inner = k > 0
        spread = jnp.where(
            (level < count[0]) & inner, mixing[jnp.maximum(k - 1, 0)], 0.0
        )
        return g, shift, terms, states, outflow, inner, spread

    def advance(step, g, shift, terms, states):
        moved_states = []
        for f, pair in enumerate(states):
            above = northward(pair[0], pair[1], row)
            below = southward(pair[0], pair[1], row)
            moved = []
            for i, c in enumerate(pair):
                if step == SPLIT_PASSES - 1 and i == 1:
                    continue
                near = roll(feed[((step * 2 + f) * 2 + i) * groups + g], shift, 1)
                moved.append(
                    apply(c, eastward(c, near), westward(c, near), above[i], below[i], terms[i])
                )
            moved_states.append(moved)
        return moved_states

    def some_levels(bottom, number, ghosts, above, carry):
        total, gain_up, gain_down, share, value_t, value_s = carry
        rows = [bottom - u for u in range(number)]
        ready = [prepare(k, ghosts, 2 * (k - above)) for k in rows]
        states = [r[3] for r in ready]
        for step in range(SPLIT_PASSES):
            states = [advance(step, *r[:3], state) for r, state in zip(ready, states)]
        for k, r, state in zip(rows, ready, states):
            outflow, inner, spread = r[4:]
            total = total + outflow
            transport = jnp.where(inner, -float(SPLIT_PASSES) * total, 0.0)
            new_down = jnp.maximum(transport, 0.0) + spread
            new_up = spread - jnp.minimum(transport, 0.0)
            pivot = (1.0 + gain_up + new_down) - gain_down * share
            inverse = 1.0 / pivot
            share = new_up * inverse
            value_t = (state[0][0] + gain_down * value_t) * inverse
            value_s = (state[1][0] + gain_down * value_s) * inverse
            gain_up, gain_down = new_up, new_down
            ratio[k] = share
            thermal_out[k] = value_t
            salty_out[k] = value_s
        return total, gain_up, gain_down, share, value_t, value_s

    carry = (jnp.zeros(TILE, jnp.float32),) * 6
    for end, start, together, ghosts in (
        (levels, SPAN, BATCH[0], (first, second)),
        (SPAN, 0, BATCH[1], (first_top, second_top)),
    ):
        carry = lax.fori_loop(
            0,
            (end - start) // together,
            lambda i, c, end=end, start=start, together=together, ghosts=ghosts: some_levels(
                end - 1 - together * i, together, ghosts, start, c
            ),
            carry,
        )

    def descend(k, carry):
        t, s = carry
        part = ratio[k]
        t = thermal_out[k] + part * t
        s = salty_out[k] + part * s
        thermal_out[k] = t
        salty_out[k] = s
        return t, s

    lax.fori_loop(1, levels, descend, (thermal_out[0], salty_out[0]))


def call(kernel, shapes, scratch=(), flags=None, direct=0, place=pltpu.HBM, shared=False):
    inner = pl.BlockSpec(memory_space=pltpu.VMEM)
    outer = pl.BlockSpec(memory_space=place)

    def run(*arrays):
        specs = [outer] * direct + [inner] * (len(arrays) - direct)
        if flags is not None:
            arrays = (flags,) + arrays
            specs = [pl.BlockSpec(memory_space=pltpu.SMEM)] + specs
        return pl.pallas_call(
            kernel,
            out_shape=tuple(jax.ShapeDtypeStruct(shape, jnp.float32) for shape in shapes),
            in_specs=specs,
            out_specs=tuple(outer if shared else inner for _ in shapes),
            scratch_shapes=list(scratch),
            input_output_aliases={1: 0, 2: 1} if shared else {},
            compiler_params=pltpu.CompilerParams(vmem_limit_bytes=32 << 20),
        )(*arrays)

    return run


def routes(lat_count, lon_count):
    first, second = [], []
    for lat in range(lat_count):
        even = (lat_count - 1 - lat) % 2 == 0
        for lon in range(lon_count):
            here = lon * lat_count + lat
            if lat == lat_count - 1:
                up = (lon_count - 1 - lon) * lat_count + lat
            else:
                up = here + 1
            down = here - 1
            (first if even else second).append((here, up))
            if lat > 0:
                (second if even else first).append((here, down))
    return first, second


def shards(
    thermal_anomaly,
    saltiness_anomaly,
    zonal_volume_flux,
    meridional_volume_flux,
    vertical_diffusion_factor,
    friction_factor,
    seawater_indicator,
    water_layer_depth,
):
    lat_count, lon_count = lax.axis_size("lat"), lax.axis_size("lon")
    lat = lax.axis_index("lat")
    levels = thermal_anomaly.shape[0]
    groups = -(-levels // SPAN)
    above = lat_count - 1 - lat
    flags = jnp.stack([1 - above % 2, (above == 0).astype(jnp.int32)]).astype(jnp.int32)
    field = (levels,) + TILE
    packed = (4 * groups + 1,) + TILE
    message = (2 * (levels - SPAN) + 1,) + TILE
    message_top = (2 * SPAN + packed[0],) + TILE

    east, north, count, pack, first, second = call(
        pack_kernel,
        (field, field, TILE, packed, message, message),
        (
            pltpu.VMEM((5,) + field, jnp.float32),
            pltpu.VMEM((2,) + TILE, jnp.int32),
            pltpu.SemaphoreType.DMA((groups + 1, 5)),
        ),
        flags=flags,
        direct=7,
    )(
        *(
            pltpu.with_memory_space_constraint(field_in, pltpu.HBM)
            for field_in in (
                thermal_anomaly,
                saltiness_anomaly,
                zonal_volume_flux,
                meridional_volume_flux,
                friction_factor,
                seawater_indicator,
                water_layer_depth,
            )
        )
    )
    first_route, second_route = routes(lat_count, lon_count)
    both = ("lon", "lat")
    first = lax.ppermute(first, both, first_route)
    second = lax.ppermute(second, both, second_route)
    ring = [(i, (i + 1) % lon_count) for i in range(lon_count)]
    from_west = lax.ppermute(pack, "lon", ring)
    from_east = lax.ppermute(pack, "lon", [(b, a) for a, b in ring])
    first_top, second_top = call(bulk_kernel, (message_top, message_top), flags=flags)(
        thermal_anomaly, saltiness_anomaly, east, north
    )
    first_top, second_top = call(
        functools.partial(corner_kernel, groups),
        (message_top, message_top),
        (pltpu.VMEM((2,) + packed, jnp.float32), pltpu.SemaphoreType.DMA((2,))),
        flags=flags,
        direct=2,
        place=pl.ANY,
        shared=True,
    )(first_top, second_top, pack, from_west, from_east)
    first_top = lax.ppermute(first_top, both, first_route)
    second_top = lax.ppermute(second_top, both, second_route)
    return call(
        step_kernel,
        (field, field),
        (
            pltpu.VMEM((16 * groups,) + TILE, jnp.float32),
            pltpu.VMEM((2 * groups,) + TILE, jnp.float32),
            pltpu.VMEM(field, jnp.float32),
        ),
        flags=flags,
    )(
        thermal_anomaly, saltiness_anomaly, east, north, vertical_diffusion_factor, count,
        first, second, first_top, second_top, pack, from_west, from_east,
    )


def solution(mesh):
    cells = P(None, "lat", "lon")
    columns = P("lat", "lon")
    return jax.shard_map(
        shards,
        mesh=mesh,
        in_specs=(cells,) * 6 + (columns,) * 2,
        out_specs=(cells, cells),
        check_vma=False,
    )
```

```python
import functools

import jax
import jax.numpy as jnp
from jax import lax
from jax.experimental import pallas as pl
from jax.experimental.pallas import tpu as pltpu
from jax.sharding import PartitionSpec as P

SPLIT_PASSES = 4
DIFFUSE = 0.05
TILE = (8, 128)
SPAN = 16
BATCH = 10, 8


def iotas():
    return (
        lax.broadcasted_iota(jnp.int32, TILE, 0),
        lax.broadcasted_iota(jnp.int32, TILE, 1),
    )


def roll(cells, shift, axis):
    return pltpu.roll(cells, shift, axis)


def flip_rows(cells, row):
    for bit in (1, 2, 4):
        cells = jnp.where((row & bit) != 0, roll(cells, bit, 0), roll(cells, 8 - bit, 0))
    return cells


def flip(cells, row, lanes):
    return flip_rows(jnp.take_along_axis(cells, lanes, axis=1), row)


def shared_tiles(t, s, e, n, natural):
    s4, n4 = roll(s, 4, 0), roll(n, 4, 0)
    return jnp.where(natural, t, s4), jnp.where(natural, e, n4)


def fold_tiles(target, number, together, row, lane):
    lanes = 127 - lane

    def some_tiles(index, carry):
        tiles = [
            flip(target[together * index + u], row, lanes) for u in range(together)
        ]
        for u, tile in enumerate(tiles):
            target[together * index + u] = -tile if u % 2 == 1 else tile
        return carry

    lax.fori_loop(0, number // together, some_tiles, 0)


def pack_kernel(
    flags, thermal, salty, zonal, meridional, friction, indicator, depth,
    east_out, north_out, count_out, pack_out, first_out,
    held, columns, arrived,
):
    levels = thermal.shape[0]
    groups = -(-levels // SPAN)
    row, lane = iotas()
    natural = (row >> 2) == flags[0]
    flat = [
        pltpu.make_async_copy(source, columns.at[i], arrived.at[groups, i])
        for i, source in enumerate((indicator, depth))
    ]
    for copy in flat:
        copy.start()
    sources = (thermal, salty, zonal, meridional, friction)
    copies = {}
    for g in reversed(range(groups)):
        part = pl.ds(SPAN * g, min(SPAN, levels - SPAN * g))
        copies[g] = [
            pltpu.make_async_copy(source.at[part], held.at[f, part], arrived.at[g, f])
            for f, source in enumerate(sources)
        ]
        for copy in copies[g]:
            copy.start()
    for copy in flat:
        copy.wait()
    count = jnp.where(columns[0] == 1, columns[1], 0).astype(jnp.float32)
    count_out[...] = count
    top_spot = 2 * (levels - SPAN)
    first_out[top_spot] = count
    spread = count
    for m in range(SPAN):
        spread = jnp.where((lane >> 3) == m, roll(count, 8 * m + 4, 1), spread)
    pack_out[4 * groups] = spread

    for g in reversed(range(groups)):
        here = min(SPAN, levels - SPAN * g)
        together = here // 2
        for copy in copies[g]:
            copy.wait()

        def pack_levels(index, packs, g=g, together=together):
            packs = list(packs)
            for u in range(together):
                m = together * index + u
                k = SPAN * g + m
                window = (lane >> 3) == m
                t, s = held[0, k], held[1, k]
                ease = 1.0 / (1.0 + held[4, k])
                e, n = held[2, k] * ease, held[3, k] * ease
                east_out[k] = e
                north_out[k] = n
                if g > 0:
                    spot = 2 * (k - SPAN)
                    first_out[spot], first_out[spot + 1] = shared_tiles(t, s, e, n, natural)
                for f, cells in enumerate((t, s, e, n)):
                    packs[f] = jnp.where(window, roll(cells, 8 * m + 4, 1), packs[f])
            return tuple(packs)

        blank = jnp.zeros(TILE, jnp.float32)
        packs = lax.fori_loop(0, 2, pack_levels, (blank,) * 4)
        for f in range(4):
            pack_out[f * groups + g] = packs[f]

    @pl.when(flags[1] == 1)
    def _():
        first_out[top_spot] = flip(count, row, 127 - lane)
        fold_tiles(first_out, top_spot, 12, row, lane)


def bulk_kernel(flags, thermal, salty, east, north, count, first_out, second_out):
    levels = thermal.shape[0]
    row, lane = iotas()
    natural = (row >> 2) == flags[0]
    other = (row >> 2) != flags[0]
    second_out[2 * levels] = count[...]

    def one_level(k, both):
        fields = thermal[k], salty[k], east[k], north[k]
        second_out[2 * k], second_out[2 * k + 1] = shared_tiles(*fields, other)
        if both:
            first_out[2 * k], first_out[2 * k + 1] = shared_tiles(*fields, natural)

    def levels_of(start, together, both, index, carry):
        for u in range(together):
            one_level(start + together * index + u, both)
        return carry

    lax.fori_loop(0, 2, functools.partial(levels_of, 0, SPAN // 2, True), 0)
    lax.fori_loop(0, (levels - SPAN) // 10, functools.partial(levels_of, SPAN, 10, False), 0)

    @pl.when(flags[1] == 1)
    def _():
        fold_tiles(first_out, 2 * SPAN, 16, row, lane)


def corner_kernel(
    groups, flags, first_in, second_in, pack, from_west, from_east,
    first_out, second_out,
    held, arrived,
):
    del first_in, second_in
    row, lane = iotas()
    natural = (row >> 2) == flags[0]
    low = (lane & 7) < 4
    size = pack.shape[0]
    for spot in range(size):
        own = pack[spot]
        left = jnp.where(low, from_west[spot], own)
        right = jnp.where(low, own, from_east[spot])
        right4 = roll(right, 4, 0)
        held[0, spot] = jnp.where(natural, left, right4)
        held[1, spot] = jnp.where(natural, right4, left)

    @pl.when(flags[1] == 1)
    def _():
        lanes = lane ^ 7
        tiles = []
        for spot in range(size):
            own = pack[spot]
            left = jnp.where(low, from_west[spot], own)
            right = jnp.where(low, own, from_east[spot])
            tile = flip(jnp.where(row < 4, roll(left, 4, 0), right), row, lanes)
            tiles.append(-tile if 2 * groups <= spot < 4 * groups else tile)
        for spot, tile in enumerate(tiles):
            held[0, spot] = tile

    copies = []
    for i, target in enumerate((first_out, second_out)):
        part = pl.ds(target.shape[0] - size, size)
        copies.append(pltpu.make_async_copy(held.at[i], target.at[part], arrived.at[i]))
    for copy in copies:
        copy.start()
    for copy in copies:
        copy.wait()


def northward(m, g, row):
    m, g = roll(m, 7, 0), roll(g, 7, 0)
    return jnp.where(row == 7, g, m), jnp.where(row == 7, m, g)


def southward(m, g, row):
    m, g = roll(m, 1, 0), roll(g, 1, 0)
    return jnp.where(row == 0, g, m), jnp.where(row == 0, m, g)


def coefficients(east, west, north, south, limits, level):
    open_east, open_west, open_north, open_south = (level < limit for limit in limits)
    leave_east = jnp.where(open_east, DIFFUSE + jnp.maximum(east, 0.0), 0.0)
    from_east = jnp.where(open_east, DIFFUSE - jnp.minimum(east, 0.0), 0.0)
    from_west = jnp.where(open_west, DIFFUSE + jnp.maximum(west, 0.0), 0.0)
    leave_west = jnp.where(open_west, DIFFUSE - jnp.minimum(west, 0.0), 0.0)
    leave_north = jnp.where(open_north, DIFFUSE + jnp.maximum(north, 0.0), 0.0)
    from_north = jnp.where(open_north, DIFFUSE - jnp.minimum(north, 0.0), 0.0)
    from_south = jnp.where(open_south, DIFFUSE + jnp.maximum(south, 0.0), 0.0)
    leave_south = jnp.where(open_south, DIFFUSE - jnp.minimum(south, 0.0), 0.0)
    stay = 1.0 - ((leave_east + leave_west) + (leave_north + leave_south))
    return stay, from_east, from_west, from_north, from_south


def apply(c, east, west, north, south, terms):
    stay, from_east, from_west, from_north, from_south = terms
    return (stay * c + (from_east * east + from_west * west)) + (
        from_north * north + from_south * south
    )


def step_kernel(
    flags, thermal, salty, east_in, north_in, mixing, count_in,
    first, first_top, second, pack, from_west, from_east,
    thermal_out, salty_out,
    feed, flow_feed, ratio,
):
    levels = thermal.shape[0]
    groups = -(-levels // SPAN)
    row, lane = iotas()
    natural = (row >> 2) == flags[0]
    top_row = (row == 7) & (flags[1] == 1)
    top_ghost = (row < 4) & (flags[1] == 1)
    low = (lane & 7) < 4
    at_west = (lane & 7) == 3

    def ghost_pair(a, b):
        return (
            jnp.where(natural, b, a),
            roll(jnp.where(natural, a, b), 4, 0),
        )

    def faces_north(n_m, n_g):
        n_up = roll(n_g, 7, 0)
        return (
            jnp.where(top_row, 0.5 * (n_m + n_up), n_m),
            jnp.where(top_ghost, n_up, n_g),
        )

    def merged(left, right):
        return jnp.where(at_west, left, roll(right, 126, 1))

    def sides(spot):
        own = pack[spot]
        left_m = jnp.where(low, from_west[spot], own)
        right_m = jnp.where(low, own, from_east[spot])
        left_g, right_g = ghost_pair(
            first_top[2 * SPAN + spot], second[2 * levels + 1 + spot]
        )
        return (left_m, left_g), (right_m, right_g)

    counts = sides(4 * groups)
    count_feed = [merged(counts[0][i], counts[1][i]) for i in range(2)]
    for g in range(groups):
        level = (SPAN * g + (lane >> 3)).astype(jnp.float32)
        fields = [sides(f * groups + g) for f in range(4)]
        states = []
        edges = []
        for side in range(2):
            (t_m, t_g), (s_m, s_g), (e_m, e_g), (n_m, n_g) = (field[side] for field in fields)
            c_m, c_g = counts[side]
            up = northward(c_m, c_g, row)
            down = southward(c_m, c_g, row)
            raw_g = e_g
            e_g = jnp.where(top_ghost, roll(e_g, 127, 1), e_g)
            face_n = faces_north(n_m, n_g)
            face_s = southward(face_n[0], face_n[1], row)
            terms = []
            for i, (c, e) in enumerate(((c_m, e_m), (c_g, e_g))):
                limits = (
                    jnp.minimum(c, roll(c, 127, 1)),
                    jnp.minimum(c, roll(c, 1, 1)),
                    jnp.minimum(c, up[i]),
                    jnp.minimum(c, down[i]),
                )
                terms.append(
                    coefficients(e, roll(e, 1, 1), face_n[i], face_s[i], limits, level)
                )
            edges.append((e_m, e_g, raw_g))
            line = []
            for pair in ((t_m, t_g), (s_m, s_g)):
                pair = [
                    jnp.where(level < c, cells, 0.0) for cells, c in zip(pair, (c_m, c_g))
                ]
                track = [pair]
                for _ in range(SPLIT_PASSES - 1):
                    above = northward(pair[0], pair[1], row)
                    below = southward(pair[0], pair[1], row)
                    pair = [
                        apply(c, roll(c, 127, 1), roll(c, 1, 1), above[i], below[i], terms[i])
                        for i, c in enumerate(pair)
                    ]
                    track.append(pair)
                line.append(track)
            states.append(line)
        flow_feed[g] = merged(edges[0][0], edges[1][0])
        flow_feed[groups + g] = merged(edges[0][1], edges[1][2])
        for step in range(SPLIT_PASSES):
            for f in range(2):
                for i in range(2):
                    feed[((step * 2 + f) * 2 + i) * groups + g] = merged(
                        states[0][f][step][i], states[1][f][step][i]
                    )

    first_lane = lane == 0
    last_lane = lane == 127

    def eastward(c, beside):
        return jnp.where(last_lane, beside, roll(c, 127, 1))

    def westward(c, beside):
        return jnp.where(first_lane, beside, roll(c, 1, 1))

    count = (
        count_in[...],
        jnp.where(natural, second[2 * levels], first[2 * (levels - SPAN)]),
    )
    count_beside = [roll(cells, 125, 1) for cells in count_feed]
    up = northward(count[0], count[1], row)
    down = southward(count[0], count[1], row)
    limits = [
        (
            jnp.minimum(count[i], eastward(count[i], count_beside[i])),
            jnp.minimum(count[i], westward(count[i], count_beside[i])),
            jnp.minimum(count[i], up[i]),
            jnp.minimum(count[i], down[i]),
        )
        for i in range(2)
    ]

    def prepare(k, firsts, spot):
        g = k >> 4
        shift = (125 - 8 * (k & 15)) & 127
        level = k.astype(jnp.float32)
        t_g, s_g = ghost_pair(firsts[spot], second[2 * k])
        e_g, n_g = ghost_pair(firsts[spot + 1], second[2 * k + 1])
        e_m, n_m = east_in[k], north_in[k]
        beside = [roll(flow_feed[i * groups + g], shift, 1) for i in range(2)]
        e_g = jnp.where(top_ghost, eastward(e_g, beside[1]), e_g)
        face_e = (e_m, e_g)
        face_w = [westward(face_e[i], beside[i]) for i in range(2)]
        face_n = faces_north(n_m, n_g)
        face_s = southward(face_n[0], face_n[1], row)
        terms = [
            coefficients(face_e[i], face_w[i], face_n[i], face_s[i], limits[i], level)
            for i in range(2)
        ]
        states = [
            [jnp.where(level < c, cells, 0.0) for cells, c in zip(pair, count)]
            for pair in ((thermal[k], t_g), (salty[k], s_g))
        ]
        open_e, open_w, open_n, open_s = (level < limit for limit in limits[0])
        outflow = (jnp.where(open_e, face_e[0], 0.0) - jnp.where(open_w, face_w[0], 0.0)) + (
            jnp.where(open_n, face_n[0], 0.0) - jnp.where(open_s, face_s[0], 0.0)
        )
        inner = k > 0
        spread = jnp.where(
            (level < count[0]) & inner, mixing[jnp.maximum(k - 1, 0)], 0.0
        )
        return g, shift, terms, states, outflow, inner, spread

    def advance(step, g, shift, terms, states):
        moved_states = []
        for f, pair in enumerate(states):
            above = northward(pair[0], pair[1], row)
            below = southward(pair[0], pair[1], row)
            moved = []
            for i, c in enumerate(pair):
                if step == SPLIT_PASSES - 1 and i == 1:
                    continue
                near = roll(feed[((step * 2 + f) * 2 + i) * groups + g], shift, 1)
                moved.append(
                    apply(c, eastward(c, near), westward(c, near), above[i], below[i], terms[i])
                )
            moved_states.append(moved)
        return moved_states

    def some_levels(bottom, number, firsts, above, carry):
        total, gain_up, gain_down, share, value_t, value_s = carry
        rows = [bottom - u for u in range(number)]
        ready = [prepare(k, firsts, 2 * (k - above)) for k in rows]
        states = [r[3] for r in ready]
        for step in range(SPLIT_PASSES):
            states = [advance(step, *r[:3], state) for r, state in zip(ready, states)]
        for k, r, state in zip(rows, ready, states):
            outflow, inner, spread = r[4:]
            total = total + outflow
            transport = jnp.where(inner, -float(SPLIT_PASSES) * total, 0.0)
            new_down = jnp.maximum(transport, 0.0) + spread
            new_up = spread - jnp.minimum(transport, 0.0)
            pivot = (1.0 + gain_up + new_down) - gain_down * share
            inverse = 1.0 / pivot
            share = new_up * inverse
            value_t = (state[0][0] + gain_down * value_t) * inverse
            value_s = (state[1][0] + gain_down * value_s) * inverse
            gain_up, gain_down = new_up, new_down
            ratio[k] = share
            thermal_out[k] = value_t
            salty_out[k] = value_s
        return total, gain_up, gain_down, share, value_t, value_s

    carry = (jnp.zeros(TILE, jnp.float32),) * 6
    for end, start, together, firsts in (
        (levels, SPAN, BATCH[0], first),
        (SPAN, 0, BATCH[1], first_top),
    ):
        carry = lax.fori_loop(
            0,
            (end - start) // together,
            lambda i, c, end=end, start=start, together=together, firsts=firsts: some_levels(
                end - 1 - together * i, together, firsts, start, c
            ),
            carry,
        )

    def descend(k, carry):
        t, s = carry
        part = ratio[k]
        t = thermal_out[k] + part * t
        s = salty_out[k] + part * s
        thermal_out[k] = t
        salty_out[k] = s
        return t, s

    lax.fori_loop(1, levels, descend, (thermal_out[0], salty_out[0]))


def call(kernel, shapes, scratch=(), flags=None, direct=0, place=pltpu.HBM, shared=False):
    inner = pl.BlockSpec(memory_space=pltpu.VMEM)
    outer = pl.BlockSpec(memory_space=place)

    def run(*arrays):
        specs = [outer] * direct + [inner] * (len(arrays) - direct)
        if flags is not None:
            arrays = (flags,) + arrays
            specs = [pl.BlockSpec(memory_space=pltpu.SMEM)] + specs
        return pl.pallas_call(
            kernel,
            out_shape=tuple(jax.ShapeDtypeStruct(shape, jnp.float32) for shape in shapes),
            in_specs=specs,
            out_specs=tuple(outer if shared else inner for _ in shapes),
            scratch_shapes=list(scratch),
            input_output_aliases={1: 0, 2: 1} if shared else {},
            compiler_params=pltpu.CompilerParams(vmem_limit_bytes=32 << 20),
        )(*arrays)

    return run


def routes(lat_count, lon_count):
    first, second = [], []
    for lat in range(lat_count):
        even = (lat_count - 1 - lat) % 2 == 0
        for lon in range(lon_count):
            here = lon * lat_count + lat
            if lat == lat_count - 1:
                up = (lon_count - 1 - lon) * lat_count + lat
            else:
                up = here + 1
            down = here - 1
            (first if even else second).append((here, up))
            if lat > 0:
                (second if even else first).append((here, down))
    return first, second


def shards(
    thermal_anomaly,
    saltiness_anomaly,
    zonal_volume_flux,
    meridional_volume_flux,
    vertical_diffusion_factor,
    friction_factor,
    seawater_indicator,
    water_layer_depth,
):
    lat_count, lon_count = lax.axis_size("lat"), lax.axis_size("lon")
    lat = lax.axis_index("lat")
    levels = thermal_anomaly.shape[0]
    groups = -(-levels // SPAN)
    above = lat_count - 1 - lat
    flags = jnp.stack([1 - above % 2, (above == 0).astype(jnp.int32)]).astype(jnp.int32)
    field = (levels,) + TILE
    packed = (4 * groups + 1,) + TILE
    message = (2 * (levels - SPAN) + 1,) + TILE
    message_top = (2 * SPAN + packed[0],) + TILE
    message_whole = (2 * levels + 1 + packed[0],) + TILE

    east, north, count, pack, first = call(
        pack_kernel,
        (field, field, TILE, packed, message),
        (
            pltpu.VMEM((5,) + field, jnp.float32),
            pltpu.VMEM((2,) + TILE, jnp.int32),
            pltpu.SemaphoreType.DMA((groups + 1, 5)),
        ),
        flags=flags,
        direct=7,
    )(
        *(
            pltpu.with_memory_space_constraint(field_in, pltpu.HBM)
            for field_in in (
                thermal_anomaly,
                saltiness_anomaly,
                zonal_volume_flux,
                meridional_volume_flux,
                friction_factor,
                seawater_indicator,
                water_layer_depth,
            )
        )
    )
    first_route, second_route = routes(lat_count, lon_count)
    both = ("lon", "lat")
    first = lax.ppermute(first, both, first_route)
    ring = [(i, (i + 1) % lon_count) for i in range(lon_count)]
    from_west = lax.ppermute(pack, "lon", ring)
    from_east = lax.ppermute(pack, "lon", [(b, a) for a, b in ring])
    first_top, second = call(bulk_kernel, (message_top, message_whole), flags=flags)(
        thermal_anomaly, saltiness_anomaly, east, north, count
    )
    first, from_west, from_east = lax.optimization_barrier((first, from_west, from_east))
    first_top, second = call(
        functools.partial(corner_kernel, groups),
        (message_top, message_whole),
        (pltpu.VMEM((2,) + packed, jnp.float32), pltpu.SemaphoreType.DMA((2,))),
        flags=flags,
        direct=2,
        place=pl.ANY,
        shared=True,
    )(first_top, second, pack, from_west, from_east)
    second = lax.ppermute(second, both, second_route)
    first_top = lax.ppermute(first_top, both, first_route)
    return call(
        step_kernel,
        (field, field),
        (
            pltpu.VMEM((16 * groups,) + TILE, jnp.float32),
            pltpu.VMEM((2 * groups,) + TILE, jnp.float32),
            pltpu.VMEM(field, jnp.float32),
        ),
        flags=flags,
    )(
        thermal_anomaly, saltiness_anomaly, east, north, vertical_diffusion_factor, count,
        first, first_top, second, pack, from_west, from_east,
    )


def solution(mesh):
    cells = P(None, "lat", "lon")
    columns = P("lat", "lon")
    return jax.shard_map(
        shards,
        mesh=mesh,
        in_specs=(cells,) * 6 + (columns,) * 2,
        out_specs=(cells, cells),
        check_vma=False,
    )
```

```python
import functools

import jax
import jax.numpy as jnp
from jax import lax
from jax.experimental import pallas as pl
from jax.experimental.pallas import tpu as pltpu
from jax.sharding import PartitionSpec as P

SPLIT_PASSES = 4
DIFFUSE = 0.05
TILE = (8, 128)
SPAN = 16
BATCH = 10, 8
FLIPS = 46


def iotas():
    return (
        lax.broadcasted_iota(jnp.int32, TILE, 0),
        lax.broadcasted_iota(jnp.int32, TILE, 1),
    )


def roll(cells, shift, axis):
    return pltpu.roll(cells, shift, axis)


def flip_rows(cells, row):
    for bit in (1, 2, 4):
        cells = jnp.where((row & bit) != 0, roll(cells, bit, 0), roll(cells, 8 - bit, 0))
    return cells


def flip(cells, row, lanes):
    return flip_rows(jnp.take_along_axis(cells, lanes, axis=1), row)


def shared_tiles(t, s, e, n, natural):
    s4, n4 = roll(s, 4, 0), roll(n, 4, 0)
    return jnp.where(natural, t, s4), jnp.where(natural, e, n4)


def fold_tiles(target, number, together, row, lane):
    lanes = 127 - lane

    def some_tiles(index, carry):
        spots = [together * index + u for u in range(together)]
        tiles = [
            -flip(target[spot], row, lanes) if u % 2 == 1 else flip(target[spot], row, lanes)
            for u, spot in enumerate(spots)
        ]
        for u, tile in enumerate(tiles):
            target[together * index + u] = tile
        return carry

    lax.fori_loop(0, number // together, some_tiles, 0)


def pack_kernel(
    flags, thermal, salty, zonal, meridional, friction, indicator, depth,
    east_out, north_out, count_out, pack_out, first_out,
    held, columns, arrived,
):
    levels = thermal.shape[0]
    groups = -(-levels // SPAN)
    row, lane = iotas()
    natural = (row >> 2) == flags[0]
    flat = [
        pltpu.make_async_copy(source, columns.at[i], arrived.at[groups, i])
        for i, source in enumerate((indicator, depth))
    ]
    for copy in flat:
        copy.start()
    sources = (thermal, salty, zonal, meridional, friction)
    copies = {}
    for g in reversed(range(groups)):
        part = pl.ds(SPAN * g, min(SPAN, levels - SPAN * g))
        copies[g] = [
            pltpu.make_async_copy(source.at[part], held.at[f, part], arrived.at[g, f])
            for f, source in enumerate(sources)
        ]
        for copy in copies[g]:
            copy.start()
    for copy in flat:
        copy.wait()
    count = jnp.where(columns[0] == 1, columns[1], 0).astype(jnp.float32)
    count_out[...] = count
    top_spot = 2 * levels
    first_out[top_spot] = count
    spread = count
    for m in range(SPAN):
        spread = jnp.where((lane >> 3) == m, roll(count, 8 * m + 4, 1), spread)
    pack_out[4 * groups] = spread

    for g in reversed(range(groups)):
        here = min(SPAN, levels - SPAN * g)
        together = here // 2
        for copy in copies[g]:
            copy.wait()

        def pack_levels(index, packs, g=g, together=together):
            packs = list(packs)
            for u in range(together):
                m = together * index + u
                k = SPAN * g + m
                window = (lane >> 3) == m
                t, s = held[0, k], held[1, k]
                ease = 1.0 / (1.0 + held[4, k])
                e, n = held[2, k] * ease, held[3, k] * ease
                east_out[k] = e
                north_out[k] = n
                first_out[2 * k], first_out[2 * k + 1] = shared_tiles(t, s, e, n, natural)
                for f, cells in enumerate((t, s, e, n)):
                    packs[f] = jnp.where(window, roll(cells, 8 * m + 4, 1), packs[f])
            return tuple(packs)

        blank = jnp.zeros(TILE, jnp.float32)
        packs = lax.fori_loop(0, 2, pack_levels, (blank,) * 4)
        for f in range(4):
            pack_out[f * groups + g] = packs[f]

    @pl.when(flags[1] == 1)
    def _():
        first_out[top_spot] = flip(count, row, 127 - lane)
        fold_tiles(first_out, top_spot, FLIPS, row, lane)


def bulk_kernel(flags, thermal, salty, east, north, count, second_out):
    levels = thermal.shape[0]
    row, lane = iotas()
    other = (row >> 2) != flags[0]
    second_out[2 * levels] = count[...]
    together = levels // 2

    def levels_of(index, carry):
        for u in range(together):
            k = together * index + u
            second_out[2 * k], second_out[2 * k + 1] = shared_tiles(
                thermal[k], salty[k], east[k], north[k], other
            )
        return carry

    lax.fori_loop(0, 2, levels_of, 0)


def corner_kernel(groups, flags, pack, from_west, from_east, first_out, second_out):
    row, lane = iotas()
    natural = (row >> 2) == flags[0]
    low = (lane & 7) < 4
    size = pack.shape[0]
    for spot in range(size):
        own = pack[spot]
        left = jnp.where(low, from_west[spot], own)
        right = jnp.where(low, own, from_east[spot])
        right4 = roll(right, 4, 0)
        first_out[spot] = jnp.where(natural, left, right4)
        second_out[spot] = jnp.where(natural, right4, left)

    @pl.when(flags[1] == 1)
    def _():
        lanes = lane ^ 7
        tiles = []
        for spot in range(size):
            own = pack[spot]
            left = jnp.where(low, from_west[spot], own)
            right = jnp.where(low, own, from_east[spot])
            tile = flip(jnp.where(row < 4, roll(left, 4, 0), right), row, lanes)
            tiles.append(-tile if 2 * groups <= spot < 4 * groups else tile)
        for spot, tile in enumerate(tiles):
            first_out[spot] = tile


def northward(m, g, row):
    m, g = roll(m, 7, 0), roll(g, 7, 0)
    return jnp.where(row == 7, g, m), jnp.where(row == 7, m, g)


def southward(m, g, row):
    m, g = roll(m, 1, 0), roll(g, 1, 0)
    return jnp.where(row == 0, g, m), jnp.where(row == 0, m, g)


def coefficients(east, west, north, south, limits, level):
    open_east, open_west, open_north, open_south = (level < limit for limit in limits)
    leave_east = jnp.where(open_east, DIFFUSE + jnp.maximum(east, 0.0), 0.0)
    from_east = jnp.where(open_east, DIFFUSE - jnp.minimum(east, 0.0), 0.0)
    from_west = jnp.where(open_west, DIFFUSE + jnp.maximum(west, 0.0), 0.0)
    leave_west = jnp.where(open_west, DIFFUSE - jnp.minimum(west, 0.0), 0.0)
    leave_north = jnp.where(open_north, DIFFUSE + jnp.maximum(north, 0.0), 0.0)
    from_north = jnp.where(open_north, DIFFUSE - jnp.minimum(north, 0.0), 0.0)
    from_south = jnp.where(open_south, DIFFUSE + jnp.maximum(south, 0.0), 0.0)
    leave_south = jnp.where(open_south, DIFFUSE - jnp.minimum(south, 0.0), 0.0)
    stay = 1.0 - ((leave_east + leave_west) + (leave_north + leave_south))
    return stay, from_east, from_west, from_north, from_south


def apply(c, east, west, north, south, terms):
    stay, from_east, from_west, from_north, from_south = terms
    return (stay * c + (from_east * east + from_west * west)) + (
        from_north * north + from_south * south
    )


def step_kernel(
    flags, thermal, salty, east_in, north_in, mixing, count_in,
    first, second, corner_first, corner_second, pack, from_west, from_east,
    thermal_out, salty_out,
    feed, flow_feed, ratio,
):
    levels = thermal.shape[0]
    groups = -(-levels // SPAN)
    row, lane = iotas()
    natural = (row >> 2) == flags[0]
    top_row = (row == 7) & (flags[1] == 1)
    top_ghost = (row < 4) & (flags[1] == 1)
    low = (lane & 7) < 4
    at_west = (lane & 7) == 3

    def ghost_pair(a, b):
        return (
            jnp.where(natural, b, a),
            roll(jnp.where(natural, a, b), 4, 0),
        )

    def faces_north(n_m, n_g):
        n_up = roll(n_g, 7, 0)
        return (
            jnp.where(top_row, 0.5 * (n_m + n_up), n_m),
            jnp.where(top_ghost, n_up, n_g),
        )

    def merged(left, right):
        return jnp.where(at_west, left, roll(right, 126, 1))

    def sides(spot):
        own = pack[spot]
        left_m = jnp.where(low, from_west[spot], own)
        right_m = jnp.where(low, own, from_east[spot])
        left_g, right_g = ghost_pair(corner_first[spot], corner_second[spot])
        return (left_m, left_g), (right_m, right_g)

    counts = sides(4 * groups)
    count_feed = [merged(counts[0][i], counts[1][i]) for i in range(2)]
    for g in range(groups):
        level = (SPAN * g + (lane >> 3)).astype(jnp.float32)
        fields = [sides(f * groups + g) for f in range(4)]
        states = []
        edges = []
        for side in range(2):
            (t_m, t_g), (s_m, s_g), (e_m, e_g), (n_m, n_g) = (field[side] for field in fields)
            c_m, c_g = counts[side]
            up = northward(c_m, c_g, row)
            down = southward(c_m, c_g, row)
            raw_g = e_g
            e_g = jnp.where(top_ghost, roll(e_g, 127, 1), e_g)
            face_n = faces_north(n_m, n_g)
            face_s = southward(face_n[0], face_n[1], row)
            terms = []
            for i, (c, e) in enumerate(((c_m, e_m), (c_g, e_g))):
                limits = (
                    jnp.minimum(c, roll(c, 127, 1)),
                    jnp.minimum(c, roll(c, 1, 1)),
                    jnp.minimum(c, up[i]),
                    jnp.minimum(c, down[i]),
                )
                terms.append(
                    coefficients(e, roll(e, 1, 1), face_n[i], face_s[i], limits, level)
                )
            edges.append((e_m, e_g, raw_g))
            line = []
            for pair in ((t_m, t_g), (s_m, s_g)):
                pair = [
                    jnp.where(level < c, cells, 0.0) for cells, c in zip(pair, (c_m, c_g))
                ]
                track = [pair]
                for _ in range(SPLIT_PASSES - 1):
                    above = northward(pair[0], pair[1], row)
                    below = southward(pair[0], pair[1], row)
                    pair = [
                        apply(c, roll(c, 127, 1), roll(c, 1, 1), above[i], below[i], terms[i])
                        for i, c in enumerate(pair)
                    ]
                    track.append(pair)
                line.append(track)
            states.append(line)
        flow_feed[g] = merged(edges[0][0], edges[1][0])
        flow_feed[groups + g] = merged(edges[0][1], edges[1][2])
        for step in range(SPLIT_PASSES):
            for f in range(2):
                for i in range(2):
                    feed[((step * 2 + f) * 2 + i) * groups + g] = merged(
                        states[0][f][step][i], states[1][f][step][i]
                    )

    first_lane = lane == 0
    last_lane = lane == 127

    def eastward(c, beside):
        return jnp.where(last_lane, beside, roll(c, 127, 1))

    def westward(c, beside):
        return jnp.where(first_lane, beside, roll(c, 1, 1))

    count = (
        count_in[...],
        jnp.where(natural, second[2 * levels], first[2 * levels]),
    )
    count_beside = [roll(cells, 125, 1) for cells in count_feed]
    up = northward(count[0], count[1], row)
    down = southward(count[0], count[1], row)
    limits = [
        (
            jnp.minimum(count[i], eastward(count[i], count_beside[i])),
            jnp.minimum(count[i], westward(count[i], count_beside[i])),
            jnp.minimum(count[i], up[i]),
            jnp.minimum(count[i], down[i]),
        )
        for i in range(2)
    ]

    def prepare(k):
        g = k >> 4
        shift = (125 - 8 * (k & 15)) & 127
        level = k.astype(jnp.float32)
        t_g, s_g = ghost_pair(first[2 * k], second[2 * k])
        e_g, n_g = ghost_pair(first[2 * k + 1], second[2 * k + 1])
        e_m, n_m = east_in[k], north_in[k]
        beside = [roll(flow_feed[i * groups + g], shift, 1) for i in range(2)]
        e_g = jnp.where(top_ghost, eastward(e_g, beside[1]), e_g)
        face_e = (e_m, e_g)
        face_w = [westward(face_e[i], beside[i]) for i in range(2)]
        face_n = faces_north(n_m, n_g)
        face_s = southward(face_n[0], face_n[1], row)
        terms = [
            coefficients(face_e[i], face_w[i], face_n[i], face_s[i], limits[i], level)
            for i in range(2)
        ]
        states = [
            [jnp.where(level < c, cells, 0.0) for cells, c in zip(pair, count)]
            for pair in ((thermal[k], t_g), (salty[k], s_g))
        ]
        open_e, open_w, open_n, open_s = (level < limit for limit in limits[0])
        outflow = (jnp.where(open_e, face_e[0], 0.0) - jnp.where(open_w, face_w[0], 0.0)) + (
            jnp.where(open_n, face_n[0], 0.0) - jnp.where(open_s, face_s[0], 0.0)
        )
        inner = k > 0
        spread = jnp.where(
            (level < count[0]) & inner, mixing[jnp.maximum(k - 1, 0)], 0.0
        )
        return g, shift, terms, states, outflow, inner, spread

    def advance(step, g, shift, terms, states):
        moved_states = []
        for f, pair in enumerate(states):
            above = northward(pair[0], pair[1], row)
            below = southward(pair[0], pair[1], row)
            moved = []
            for i, c in enumerate(pair):
                if step == SPLIT_PASSES - 1 and i == 1:
                    continue
                near = roll(feed[((step * 2 + f) * 2 + i) * groups + g], shift, 1)
                moved.append(
                    apply(c, eastward(c, near), westward(c, near), above[i], below[i], terms[i])
                )
            moved_states.append(moved)
        return moved_states

    def some_levels(bottom, number, carry):
        total, gain_up, gain_down, share, value_t, value_s = carry
        rows = [bottom - u for u in range(number)]
        ready = [prepare(k) for k in rows]
        states = [r[3] for r in ready]
        for step in range(SPLIT_PASSES):
            states = [advance(step, *r[:3], state) for r, state in zip(ready, states)]
        for k, r, state in zip(rows, ready, states):
            outflow, inner, spread = r[4:]
            total = total + outflow
            transport = jnp.where(inner, -float(SPLIT_PASSES) * total, 0.0)
            new_down = jnp.maximum(transport, 0.0) + spread
            new_up = spread - jnp.minimum(transport, 0.0)
            pivot = (1.0 + gain_up + new_down) - gain_down * share
            inverse = 1.0 / pivot
            share = new_up * inverse
            value_t = (state[0][0] + gain_down * value_t) * inverse
            value_s = (state[1][0] + gain_down * value_s) * inverse
            gain_up, gain_down = new_up, new_down
            ratio[k] = share
            thermal_out[k] = value_t
            salty_out[k] = value_s
        return total, gain_up, gain_down, share, value_t, value_s

    carry = (jnp.zeros(TILE, jnp.float32),) * 6
    for end, start, together in ((levels, SPAN, BATCH[0]), (SPAN, 0, BATCH[1])):
        carry = lax.fori_loop(
            0,
            (end - start) // together,
            lambda i, c, end=end, together=together: some_levels(
                end - 1 - together * i, together, c
            ),
            carry,
        )

    def descend(k, carry):
        t, s = carry
        part = ratio[k]
        t = thermal_out[k] + part * t
        s = salty_out[k] + part * s
        thermal_out[k] = t
        salty_out[k] = s
        return t, s

    lax.fori_loop(1, levels, descend, (thermal_out[0], salty_out[0]))


def call(kernel, shapes, scratch=(), flags=None, direct=0):
    inner = pl.BlockSpec(memory_space=pltpu.VMEM)
    outer = pl.BlockSpec(memory_space=pltpu.HBM)

    def run(*arrays):
        return pl.pallas_call(
            kernel,
            out_shape=tuple(jax.ShapeDtypeStruct(shape, jnp.float32) for shape in shapes),
            in_specs=[pl.BlockSpec(memory_space=pltpu.SMEM)]
            + [outer] * direct
            + [inner] * (len(arrays) - direct),
            out_specs=tuple(inner for _ in shapes),
            scratch_shapes=list(scratch),
            compiler_params=pltpu.CompilerParams(vmem_limit_bytes=32 << 20),
        )(flags, *arrays)

    return run


def routes(lat_count, lon_count):
    first, second = [], []
    for lat in range(lat_count):
        even = (lat_count - 1 - lat) % 2 == 0
        for lon in range(lon_count):
            here = lon * lat_count + lat
            if lat == lat_count - 1:
                up = (lon_count - 1 - lon) * lat_count + lat
            else:
                up = here + 1
            down = here - 1
            (first if even else second).append((here, up))
            if lat > 0:
                (second if even else first).append((here, down))
    return first, second


def shards(
    thermal_anomaly,
    saltiness_anomaly,
    zonal_volume_flux,
    meridional_volume_flux,
    vertical_diffusion_factor,
    friction_factor,
    seawater_indicator,
    water_layer_depth,
):
    lat_count, lon_count = lax.axis_size("lat"), lax.axis_size("lon")
    lat = lax.axis_index("lat")
    levels = thermal_anomaly.shape[0]
    groups = -(-levels // SPAN)
    above = lat_count - 1 - lat
    flags = jnp.stack([1 - above % 2, (above == 0).astype(jnp.int32)]).astype(jnp.int32)
    field = (levels,) + TILE
    packed = (4 * groups + 1,) + TILE
    message = (2 * levels + 1,) + TILE

    east, north, count, pack, first = call(
        pack_kernel,
        (field, field, TILE, packed, message),
        (
            pltpu.VMEM((5,) + field, jnp.float32),
            pltpu.VMEM((2,) + TILE, jnp.int32),
            pltpu.SemaphoreType.DMA((groups + 1, 5)),
        ),
        flags=flags,
        direct=7,
    )(
        *(
            pltpu.with_memory_space_constraint(field_in, pltpu.HBM)
            for field_in in (
                thermal_anomaly,
                saltiness_anomaly,
                zonal_volume_flux,
                meridional_volume_flux,
                friction_factor,
                seawater_indicator,
                water_layer_depth,
            )
        )
    )
    first_route, second_route = routes(lat_count, lon_count)
    both = ("lon", "lat")
    first = lax.ppermute(first, both, first_route)
    ring = [(i, (i + 1) % lon_count) for i in range(lon_count)]
    from_west = lax.ppermute(pack, "lon", ring)
    from_east = lax.ppermute(pack, "lon", [(b, a) for a, b in ring])
    (second,) = call(bulk_kernel, (message,), flags=flags)(
        thermal_anomaly, saltiness_anomaly, east, north, count
    )
    second = lax.ppermute(second, both, second_route)
    corner_first, corner_second = call(
        functools.partial(corner_kernel, groups), (packed, packed), flags=flags
    )(pack, from_west, from_east)
    corner_first = lax.ppermute(corner_first, both, first_route)
    corner_second = lax.ppermute(corner_second, both, second_route)
    return call(
        step_kernel,
        (field, field),
        (
            pltpu.VMEM((16 * groups,) + TILE, jnp.float32),
            pltpu.VMEM((2 * groups,) + TILE, jnp.float32),
            pltpu.VMEM(field, jnp.float32),
        ),
        flags=flags,
    )(
        thermal_anomaly, saltiness_anomaly, east, north, vertical_diffusion_factor, count,
        first, second, corner_first, corner_second, pack, from_west, from_east,
    )


def solution(mesh):
    cells = P(None, "lat", "lon")
    columns = P("lat", "lon")
    return jax.shard_map(
        shards,
        mesh=mesh,
        in_specs=(cells,) * 6 + (columns,) * 2,
        out_specs=(cells, cells),
        check_vma=False,
    )
```

```python
import functools

import jax
import jax.numpy as jnp
from jax import lax
from jax.experimental import pallas as pl
from jax.experimental.pallas import tpu as pltpu
from jax.sharding import PartitionSpec as P

SPLIT_PASSES = 4
DIFFUSE = 0.05
TILE = (8, 128)
SPAN = 16
BATCH = 10, 8
CHUNK = 12
FLIPS = 46


def iotas():
    return (
        lax.broadcasted_iota(jnp.int32, TILE, 0),
        lax.broadcasted_iota(jnp.int32, TILE, 1),
    )


def roll(cells, shift, axis):
    return pltpu.roll(cells, shift, axis)


def flip_rows(cells, row):
    for bit in (1, 2, 4):
        cells = jnp.where((row & bit) != 0, roll(cells, bit, 0), roll(cells, 8 - bit, 0))
    return cells


def flip(cells, row, lanes):
    return flip_rows(jnp.take_along_axis(cells, lanes, axis=1), row)


def shared_tiles(t, s, e, n, natural):
    s4, n4 = roll(s, 4, 0), roll(n, 4, 0)
    return jnp.where(natural, t, s4), jnp.where(natural, e, n4)


def pack_kernel(
    flags, thermal, salty, zonal, meridional, friction, indicator, depth,
    east_out, north_out, count_out, pack_out, first_out, second_out,
    held, columns, arrived,
):
    levels = thermal.shape[0]
    groups = -(-levels // SPAN)
    row, lane = iotas()
    natural = (row >> 2) == flags[0]
    other = (row >> 2) != flags[0]
    flat = [
        pltpu.make_async_copy(source, columns.at[i], arrived.at[groups, i])
        for i, source in enumerate((indicator, depth))
    ]
    for copy in flat:
        copy.start()
    sources = (thermal, salty, zonal, meridional, friction)
    copies = {}
    for g in reversed(range(groups)):
        part = pl.ds(SPAN * g, min(SPAN, levels - SPAN * g))
        copies[g] = [
            pltpu.make_async_copy(source.at[part], held.at[f, part], arrived.at[g, f])
            for f, source in enumerate(sources)
        ]
        for copy in copies[g]:
            copy.start()
    for copy in flat:
        copy.wait()
    count = jnp.where(columns[0] == 1, columns[1], 0).astype(jnp.float32)
    count_out[...] = count
    top_spot = 2 * levels
    first_out[top_spot] = count
    second_out[top_spot] = count
    spread = count
    for m in range(SPAN):
        spread = jnp.where((lane >> 3) == m, roll(count, 8 * m + 4, 1), spread)
    pack_out[4 * groups] = spread

    for g in reversed(range(groups)):
        here = min(SPAN, levels - SPAN * g)
        together = here // 2
        for copy in copies[g]:
            copy.wait()

        def pack_levels(index, packs, g=g, together=together):
            packs = list(packs)
            for u in range(together):
                m = together * index + u
                k = SPAN * g + m
                window = (lane >> 3) == m
                t, s = held[0, k], held[1, k]
                ease = 1.0 / (1.0 + held[4, k])
                e, n = held[2, k] * ease, held[3, k] * ease
                east_out[k] = e
                north_out[k] = n
                first_out[2 * k], first_out[2 * k + 1] = shared_tiles(t, s, e, n, natural)
                second_out[2 * k], second_out[2 * k + 1] = shared_tiles(t, s, e, n, other)
                for f, cells in enumerate((t, s, e, n)):
                    packs[f] = jnp.where(window, roll(cells, 8 * m + 4, 1), packs[f])
            return tuple(packs)

        blank = jnp.zeros(TILE, jnp.float32)
        packs = lax.fori_loop(0, 2, pack_levels, (blank,) * 4)
        for f in range(4):
            pack_out[f * groups + g] = packs[f]


def corner_kernel(
    groups, flags, from_west, from_east, bulk, first_out, second_out, fold_out
):
    row, lane = iotas()
    natural = (row >> 2) == flags[0]
    other = (row >> 2) != flags[0]
    low = (lane & 7) < 4

    def beside(spot):
        return jnp.where(low, from_west[spot], from_east[spot])

    tiles = []
    for g in range(groups):
        fields = [beside(f * groups + g) for f in range(4)]
        tiles += shared_tiles(*fields, natural)
        second_out[2 * g], second_out[2 * g + 1] = shared_tiles(*fields, other)
    tiles.append(beside(4 * groups))
    second_out[2 * groups] = tiles[-1]
    for spot, tile in enumerate(tiles):
        first_out[spot] = tile

    @pl.when(flags[1] == 1)
    def _():
        for spot, tile in enumerate(tiles):
            tile = flip(tile, row, lane ^ 7)
            first_out[spot] = -tile if spot % 2 == 1 else tile
        lanes = 127 - lane
        last = bulk.shape[0] - 1
        fold_out[last] = flip(bulk[last], row, lanes)

        def some_tiles(index, carry):
            for u in range(FLIPS):
                spot = FLIPS * index + u
                tile = flip(bulk[spot], row, lanes)
                fold_out[spot] = -tile if u % 2 == 1 else tile
            return carry

        lax.fori_loop(0, last // FLIPS, some_tiles, 0)


def northward(m, g, row):
    m, g = roll(m, 7, 0), roll(g, 7, 0)
    return jnp.where(row == 7, g, m), jnp.where(row == 7, m, g)


def southward(m, g, row):
    m, g = roll(m, 1, 0), roll(g, 1, 0)
    return jnp.where(row == 0, g, m), jnp.where(row == 0, m, g)


def coefficients(east, west, north, south, limits, level):
    open_east, open_west, open_north, open_south = (level < limit for limit in limits)
    leave_east = jnp.where(open_east, DIFFUSE + jnp.maximum(east, 0.0), 0.0)
    from_east = jnp.where(open_east, DIFFUSE - jnp.minimum(east, 0.0), 0.0)
    from_west = jnp.where(open_west, DIFFUSE + jnp.maximum(west, 0.0), 0.0)
    leave_west = jnp.where(open_west, DIFFUSE - jnp.minimum(west, 0.0), 0.0)
    leave_north = jnp.where(open_north, DIFFUSE + jnp.maximum(north, 0.0), 0.0)
    from_north = jnp.where(open_north, DIFFUSE - jnp.minimum(north, 0.0), 0.0)
    from_south = jnp.where(open_south, DIFFUSE + jnp.maximum(south, 0.0), 0.0)
    leave_south = jnp.where(open_south, DIFFUSE - jnp.minimum(south, 0.0), 0.0)
    stay = 1.0 - ((leave_east + leave_west) + (leave_north + leave_south))
    return stay, from_east, from_west, from_north, from_south


def apply(c, east, west, north, south, terms):
    stay, from_east, from_west, from_north, from_south = terms
    return (stay * c + (from_east * east + from_west * west)) + (
        from_north * north + from_south * south
    )


def step_kernel(
    flags, thermal, salty, east_in, north_in, mixing, count_in,
    first, second, fold, corner_first, corner_second, pack, from_west, from_east,
    thermal_out, salty_out,
    feed, flow_feed, ratio, solved, sent,
):
    levels = thermal.shape[0]
    groups = -(-levels // SPAN)
    row, lane = iotas()
    natural = (row >> 2) == flags[0]
    is_top = (flags[1] + 0 * row) == 1
    top_row = (row == 7) & is_top
    top_ghost = (row < 4) & is_top
    low = (lane & 7) < 4
    at_west = (lane & 7) == 3

    def ghost_pair(a, b):
        return (
            jnp.where(natural, b, a),
            roll(jnp.where(natural, a, b), 4, 0),
        )

    def faces_north(n_m, n_g):
        n_up = roll(n_g, 7, 0)
        return (
            jnp.where(top_row, 0.5 * (n_m + n_up), n_m),
            jnp.where(top_ghost, n_up, n_g),
        )

    def ghosts(spot):
        return ghost_pair(jnp.where(is_top, fold[spot], first[spot]), second[spot])

    def merged(left, right):
        return jnp.where(at_west, left, roll(right, 126, 1))

    def sides(own_m, own_g, spot, beside_g):
        return (
            (
                jnp.where(low, from_west[spot], own_m),
                jnp.where(low, beside_g, own_g),
            ),
            (
                jnp.where(low, own_m, from_east[spot]),
                jnp.where(low, own_g, beside_g),
            ),
        )

    def edge_columns(g):
        edges = [jnp.zeros(TILE, jnp.float32)] * 4
        for m in range(min(SPAN, levels - SPAN * g)):
            spot = 2 * (SPAN * g + m)
            window = (lane >> 3) == m
            for f, cells in enumerate((*ghosts(spot), *ghosts(spot + 1))):
                edges[f] = jnp.where(window, roll(cells, 8 * m + 4, 1), edges[f])
        return edges

    ghost_count = ghosts(2 * levels)[0]
    edge_count = ghost_count
    for m in range(SPAN):
        edge_count = jnp.where(
            (lane >> 3) == m, roll(ghost_count, 8 * m + 4, 1), edge_count
        )
    counts = sides(
        pack[4 * groups],
        edge_count,
        4 * groups,
        ghost_pair(corner_first[2 * groups], corner_second[2 * groups])[0],
    )
    count_feed = [merged(counts[0][i], counts[1][i]) for i in range(2)]
    for g in range(groups):
        level = (SPAN * g + (lane >> 3)).astype(jnp.float32)
        edge = edge_columns(g)
        beside_g = [
            cells
            for i in range(2)
            for cells in ghost_pair(corner_first[2 * g + i], corner_second[2 * g + i])
        ]
        fields = [
            sides(pack[f * groups + g], edge[f], f * groups + g, beside_g[f])
            for f in range(4)
        ]
        states = []
        edges = []
        for side in range(2):
            (t_m, t_g), (s_m, s_g), (e_m, e_g), (n_m, n_g) = (field[side] for field in fields)
            c_m, c_g = counts[side]
            up = northward(c_m, c_g, row)
            down = southward(c_m, c_g, row)
            raw_g = e_g
            e_g = jnp.where(top_ghost, roll(e_g, 127, 1), e_g)
            face_n = faces_north(n_m, n_g)
            face_s = southward(face_n[0], face_n[1], row)
            terms = []
            for i, (c, e) in enumerate(((c_m, e_m), (c_g, e_g))):
                limits = (
                    jnp.minimum(c, roll(c, 127, 1)),
                    jnp.minimum(c, roll(c, 1, 1)),
                    jnp.minimum(c, up[i]),
                    jnp.minimum(c, down[i]),
                )
                terms.append(
                    coefficients(e, roll(e, 1, 1), face_n[i], face_s[i], limits, level)
                )
            edges.append((e_m, e_g, raw_g))
            line = []
            for pair in ((t_m, t_g), (s_m, s_g)):
                pair = [
                    jnp.where(level < c, cells, 0.0) for cells, c in zip(pair, (c_m, c_g))
                ]
                track = [pair]
                for _ in range(SPLIT_PASSES - 1):
                    above = northward(pair[0], pair[1], row)
                    below = southward(pair[0], pair[1], row)
                    pair = [
                        apply(c, roll(c, 127, 1), roll(c, 1, 1), above[i], below[i], terms[i])
                        for i, c in enumerate(pair)
                    ]
                    track.append(pair)
                line.append(track)
            states.append(line)
        flow_feed[g] = merged(edges[0][0], edges[1][0])
        flow_feed[groups + g] = merged(edges[0][1], edges[1][2])
        for step in range(SPLIT_PASSES):
            for f in range(2):
                for i in range(2):
                    feed[((step * 2 + f) * 2 + i) * groups + g] = merged(
                        states[0][f][step][i], states[1][f][step][i]
                    )

    first_lane = lane == 0
    last_lane = lane == 127

    def eastward(c, beside):
        return jnp.where(last_lane, beside, roll(c, 127, 1))

    def westward(c, beside):
        return jnp.where(first_lane, beside, roll(c, 1, 1))

    count = (
        count_in[...],
        ghost_count,
    )
    count_beside = [roll(cells, 125, 1) for cells in count_feed]
    up = northward(count[0], count[1], row)
    down = southward(count[0], count[1], row)
    limits = [
        (
            jnp.minimum(count[i], eastward(count[i], count_beside[i])),
            jnp.minimum(count[i], westward(count[i], count_beside[i])),
            jnp.minimum(count[i], up[i]),
            jnp.minimum(count[i], down[i]),
        )
        for i in range(2)
    ]

    def prepare(k):
        g = k >> 4
        shift = (125 - 8 * (k & 15)) & 127
        level = k.astype(jnp.float32)
        t_g, s_g = ghosts(2 * k)
        e_g, n_g = ghosts(2 * k + 1)
        e_m, n_m = east_in[k], north_in[k]
        beside = [roll(flow_feed[i * groups + g], shift, 1) for i in range(2)]
        e_g = jnp.where(top_ghost, eastward(e_g, beside[1]), e_g)
        face_e = (e_m, e_g)
        face_w = [westward(face_e[i], beside[i]) for i in range(2)]
        face_n = faces_north(n_m, n_g)
        face_s = southward(face_n[0], face_n[1], row)
        terms = [
            coefficients(face_e[i], face_w[i], face_n[i], face_s[i], limits[i], level)
            for i in range(2)
        ]
        states = [
            [jnp.where(level < c, cells, 0.0) for cells, c in zip(pair, count)]
            for pair in ((thermal[k], t_g), (salty[k], s_g))
        ]
        open_e, open_w, open_n, open_s = (level < limit for limit in limits[0])
        outflow = (jnp.where(open_e, face_e[0], 0.0) - jnp.where(open_w, face_w[0], 0.0)) + (
            jnp.where(open_n, face_n[0], 0.0) - jnp.where(open_s, face_s[0], 0.0)
        )
        inner = k > 0
        spread = jnp.where(
            (level < count[0]) & inner, mixing[jnp.maximum(k - 1, 0)], 0.0
        )
        return g, shift, terms, states, outflow, inner, spread

    def advance(step, g, shift, terms, states):
        moved_states = []
        for f, pair in enumerate(states):
            above = northward(pair[0], pair[1], row)
            below = southward(pair[0], pair[1], row)
            moved = []
            for i, c in enumerate(pair):
                if step == SPLIT_PASSES - 1 and i == 1:
                    continue
                near = roll(feed[((step * 2 + f) * 2 + i) * groups + g], shift, 1)
                moved.append(
                    apply(c, eastward(c, near), westward(c, near), above[i], below[i], terms[i])
                )
            moved_states.append(moved)
        return moved_states

    def some_levels(bottom, number, carry):
        total, gain_up, gain_down, share, value_t, value_s = carry
        rows = [bottom - u for u in range(number)]
        ready = [prepare(k) for k in rows]
        states = [r[3] for r in ready]
        for step in range(SPLIT_PASSES):
            states = [advance(step, *r[:3], state) for r, state in zip(ready, states)]
        for k, r, state in zip(rows, ready, states):
            outflow, inner, spread = r[4:]
            total = total + outflow
            transport = jnp.where(inner, -float(SPLIT_PASSES) * total, 0.0)
            new_down = jnp.maximum(transport, 0.0) + spread
            new_up = spread - jnp.minimum(transport, 0.0)
            pivot = (1.0 + gain_up + new_down) - gain_down * share
            inverse = 1.0 / pivot
            share = new_up * inverse
            value_t = (state[0][0] + gain_down * value_t) * inverse
            value_s = (state[1][0] + gain_down * value_s) * inverse
            gain_up, gain_down = new_up, new_down
            ratio[k] = share
            solved[0, k] = value_t
            solved[1, k] = value_s
        return total, gain_up, gain_down, share, value_t, value_s

    carry = (jnp.zeros(TILE, jnp.float32),) * 6
    for end, start, together in ((levels, SPAN, BATCH[0]), (SPAN, 0, BATCH[1])):
        carry = lax.fori_loop(
            0,
            (end - start) // together,
            lambda i, c, end=end, together=together: some_levels(
                end - 1 - together * i, together, c
            ),
            carry,
        )

    t, s = solved[0, 0], solved[1, 0]
    copies = []
    for start in range(0, levels, CHUNK):
        end = min(start + CHUNK, levels)
        for k in range(max(start, 1), end):
            part = ratio[k]
            t = solved[0, k] + part * t
            s = solved[1, k] + part * s
            solved[0, k] = t
            solved[1, k] = s
        part = pl.ds(start, end - start)
        for i, target in enumerate((thermal_out, salty_out)):
            copies.append(
                pltpu.make_async_copy(
                    solved.at[i, part], target.at[part], sent.at[start // CHUNK, i]
                )
            )
            copies[-1].start()
    for copy in copies:
        copy.wait()


def call(kernel, shapes, scratch=(), flags=None, direct=0, out=pltpu.VMEM):
    inner = pl.BlockSpec(memory_space=pltpu.VMEM)
    outer = pl.BlockSpec(memory_space=pltpu.HBM)

    def run(*arrays):
        return pl.pallas_call(
            kernel,
            out_shape=tuple(jax.ShapeDtypeStruct(shape, jnp.float32) for shape in shapes),
            in_specs=[pl.BlockSpec(memory_space=pltpu.SMEM)]
            + [outer] * direct
            + [inner] * (len(arrays) - direct),
            out_specs=tuple(pl.BlockSpec(memory_space=out) for _ in shapes),
            scratch_shapes=list(scratch),
            compiler_params=pltpu.CompilerParams(vmem_limit_bytes=32 << 20),
        )(flags, *arrays)

    return run


def routes(lat_count, lon_count):
    first, second, fold = [], [], []
    for lat in range(lat_count):
        even = (lat_count - 1 - lat) % 2 == 0
        for lon in range(lon_count):
            here = lon * lat_count + lat
            if lat == lat_count - 1:
                fold.append((here, (lon_count - 1 - lon) * lat_count + lat))
            else:
                (first if even else second).append((here, here + 1))
            if lat > 0:
                (second if even else first).append((here, here - 1))
    return first, second, fold


def shards(
    thermal_anomaly,
    saltiness_anomaly,
    zonal_volume_flux,
    meridional_volume_flux,
    vertical_diffusion_factor,
    friction_factor,
    seawater_indicator,
    water_layer_depth,
):
    lat_count, lon_count = lax.axis_size("lat"), lax.axis_size("lon")
    lat = lax.axis_index("lat")
    levels = thermal_anomaly.shape[0]
    groups = -(-levels // SPAN)
    above = lat_count - 1 - lat
    flags = jnp.stack([1 - above % 2, (above == 0).astype(jnp.int32)]).astype(jnp.int32)
    field = (levels,) + TILE
    packed = (4 * groups + 1,) + TILE
    message = (2 * levels + 1,) + TILE
    corner = (2 * groups + 1,) + TILE

    east, north, count, pack, first, second = call(
        pack_kernel,
        (field, field, TILE, packed, message, message),
        (
            pltpu.VMEM((5,) + field, jnp.float32),
            pltpu.VMEM((2,) + TILE, jnp.int32),
            pltpu.SemaphoreType.DMA((groups + 1, 5)),
        ),
        flags=flags,
        direct=7,
    )(
        *(
            pltpu.with_memory_space_constraint(field_in, pltpu.HBM)
            for field_in in (
                thermal_anomaly,
                saltiness_anomaly,
                zonal_volume_flux,
                meridional_volume_flux,
                friction_factor,
                seawater_indicator,
                water_layer_depth,
            )
        )
    )
    first_route, second_route, fold_route = routes(lat_count, lon_count)
    both = ("lon", "lat")
    message_first = lax.ppermute(first, both, first_route)
    second = lax.ppermute(second, both, second_route)
    ring = [(i, (i + 1) % lon_count) for i in range(lon_count)]
    from_west = lax.ppermute(pack, "lon", ring)
    from_east = lax.ppermute(pack, "lon", [(b, a) for a, b in ring])
    corner_first, corner_second, fold = call(
        functools.partial(corner_kernel, groups), (corner, corner, message), flags=flags
    )(from_west, from_east, first)
    fold = lax.ppermute(fold, both, fold_route)
    corner_first = lax.ppermute(corner_first, both, first_route + fold_route)
    corner_second = lax.ppermute(corner_second, both, second_route)
    return call(
        step_kernel,
        (field, field),
        (
            pltpu.VMEM((16 * groups,) + TILE, jnp.float32),
            pltpu.VMEM((2 * groups,) + TILE, jnp.float32),
            pltpu.VMEM(field, jnp.float32),
            pltpu.VMEM((2,) + field, jnp.float32),
            pltpu.SemaphoreType.DMA((-(-levels // CHUNK), 2)),
        ),
        flags=flags,
        out=pltpu.HBM,
    )(
        thermal_anomaly, saltiness_anomaly, east, north, vertical_diffusion_factor, count,
        message_first, second, fold, corner_first, corner_second, pack, from_west, from_east,
    )


def solution(mesh):
    cells = P(None, "lat", "lon")
    columns = P("lat", "lon")
    return jax.shard_map(
        shards,
        mesh=mesh,
        in_specs=(cells,) * 6 + (columns,) * 2,
        out_specs=(cells, cells),
        check_vma=False,
    )
```

```python
import functools

import jax
import jax.numpy as jnp
from jax import lax
from jax.experimental import pallas as pl
from jax.experimental.pallas import tpu as pltpu
from jax.sharding import PartitionSpec as P

SPLIT_PASSES = 4
DIFFUSE = 0.05
TILE = (8, 128)
SPAN = 16
BATCH = 10, 8
CHUNK = 12
FLIPS = 46


def iotas():
    return (
        lax.broadcasted_iota(jnp.int32, TILE, 0),
        lax.broadcasted_iota(jnp.int32, TILE, 1),
    )


def roll(cells, shift, axis):
    return pltpu.roll(cells, shift, axis)


def flip_rows(cells, row):
    for bit in (1, 2, 4):
        cells = jnp.where((row & bit) != 0, roll(cells, bit, 0), roll(cells, 8 - bit, 0))
    return cells


def flip(cells, row, lanes):
    return flip_rows(jnp.take_along_axis(cells, lanes, axis=1), row)


def shared_tiles(t, s, e, n, natural):
    s4, n4 = roll(s, 4, 0), roll(n, 4, 0)
    return jnp.where(natural, t, s4), jnp.where(natural, e, n4)


def pack_kernel(
    flags, thermal, salty, zonal, meridional, friction, indicator, depth,
    east_out, north_out, count_out, pack_out, first_out, second_out,
    held, columns, arrived,
):
    levels = thermal.shape[0]
    groups = -(-levels // SPAN)
    row, lane = iotas()
    natural = (row >> 2) == flags[0]
    other = (row >> 2) != flags[0]
    flat = [
        pltpu.make_async_copy(source, columns.at[i], arrived.at[groups, i])
        for i, source in enumerate((indicator, depth))
    ]
    for copy in flat:
        copy.start()
    sources = (thermal, salty, zonal, meridional, friction)
    copies = {}
    for g in reversed(range(groups)):
        part = pl.ds(SPAN * g, min(SPAN, levels - SPAN * g))
        copies[g] = [
            pltpu.make_async_copy(source.at[part], held.at[f, part], arrived.at[g, f])
            for f, source in enumerate(sources)
        ]
        for copy in copies[g]:
            copy.start()
    for copy in flat:
        copy.wait()
    count = jnp.where(columns[0] == 1, columns[1], 0).astype(jnp.float32)
    count_out[...] = count
    top_spot = 2 * levels
    first_out[top_spot] = count
    second_out[top_spot] = count
    spread = count
    for m in range(SPAN):
        spread = jnp.where((lane >> 3) == m, roll(count, 8 * m + 4, 1), spread)
    pack_out[4 * groups] = spread

    for g in reversed(range(groups)):
        here = min(SPAN, levels - SPAN * g)
        together = here // 2
        for copy in copies[g]:
            copy.wait()

        def pack_levels(index, packs, g=g, together=together):
            packs = list(packs)
            for u in range(together):
                m = together * index + u
                k = SPAN * g + m
                window = (lane >> 3) == m
                t, s = held[0, k], held[1, k]
                ease = 1.0 / (1.0 + held[4, k])
                e, n = held[2, k] * ease, held[3, k] * ease
                east_out[k] = e
                north_out[k] = n
                first_out[2 * k], first_out[2 * k + 1] = shared_tiles(t, s, e, n, natural)
                second_out[2 * k], second_out[2 * k + 1] = shared_tiles(t, s, e, n, other)
                for f, cells in enumerate((t, s, e, n)):
                    packs[f] = jnp.where(window, roll(cells, 8 * m + 4, 1), packs[f])
            return tuple(packs)

        blank = jnp.zeros(TILE, jnp.float32)
        packs = lax.fori_loop(0, 2, pack_levels, (blank,) * 4)
        for f in range(4):
            pack_out[f * groups + g] = packs[f]


def corner_kernel(
    groups, flags, from_west, from_east, bulk, first_out, second_out, fold_out
):
    row, lane = iotas()
    natural = (row >> 2) == flags[0]
    other = (row >> 2) != flags[0]
    low = (lane & 7) < 4

    def beside(spot):
        return jnp.where(low, from_west[spot], from_east[spot])

    tiles = []
    for g in range(groups):
        fields = [beside(f * groups + g) for f in range(4)]
        tiles += shared_tiles(*fields, natural)
        second_out[2 * g], second_out[2 * g + 1] = shared_tiles(*fields, other)
    tiles.append(beside(4 * groups))
    second_out[2 * groups] = tiles[-1]
    for spot, tile in enumerate(tiles):
        first_out[spot] = tile

    @pl.when(flags[1] == 1)
    def _():
        for spot, tile in enumerate(tiles):
            tile = flip(tile, row, lane ^ 7)
            first_out[spot] = -tile if spot % 2 == 1 else tile
        lanes = 127 - lane
        last = bulk.shape[0] - 1
        fold_out[last] = flip(bulk[last], row, lanes)

        def some_tiles(index, carry):
            for u in range(FLIPS):
                spot = FLIPS * index + u
                tile = flip(bulk[spot], row, lanes)
                fold_out[spot] = -tile if u % 2 == 1 else tile
            return carry

        lax.fori_loop(0, last // FLIPS, some_tiles, 0)


def northward(m, g, row):
    m, g = roll(m, 7, 0), roll(g, 7, 0)
    return jnp.where(row == 7, g, m), jnp.where(row == 7, m, g)


def southward(m, g, row):
    m, g = roll(m, 1, 0), roll(g, 1, 0)
    return jnp.where(row == 0, g, m), jnp.where(row == 0, m, g)


def coefficients(east, west, north, south, limits, level):
    open_east, open_west, open_north, open_south = (level < limit for limit in limits)
    leave_east = jnp.where(open_east, DIFFUSE + jnp.maximum(east, 0.0), 0.0)
    from_east = jnp.where(open_east, DIFFUSE - jnp.minimum(east, 0.0), 0.0)
    from_west = jnp.where(open_west, DIFFUSE + jnp.maximum(west, 0.0), 0.0)
    leave_west = jnp.where(open_west, DIFFUSE - jnp.minimum(west, 0.0), 0.0)
    leave_north = jnp.where(open_north, DIFFUSE + jnp.maximum(north, 0.0), 0.0)
    from_north = jnp.where(open_north, DIFFUSE - jnp.minimum(north, 0.0), 0.0)
    from_south = jnp.where(open_south, DIFFUSE + jnp.maximum(south, 0.0), 0.0)
    leave_south = jnp.where(open_south, DIFFUSE - jnp.minimum(south, 0.0), 0.0)
    stay = 1.0 - ((leave_east + leave_west) + (leave_north + leave_south))
    return stay, from_east, from_west, from_north, from_south


def apply(c, east, west, north, south, terms):
    stay, from_east, from_west, from_north, from_south = terms
    return (stay * c + (from_east * east + from_west * west)) + (
        from_north * north + from_south * south
    )


def edge_kernel(flags, first, second, fold, edge_out):
    levels = first.shape[0] // 2
    groups = -(-levels // SPAN)
    row, lane = iotas()
    natural = (row >> 2) == flags[0]
    is_top = (flags[1] + 0 * row) == 1

    def ghosts(spot):
        a = jnp.where(is_top, fold[spot], first[spot])
        b = second[spot]
        return jnp.where(natural, b, a), roll(jnp.where(natural, a, b), 4, 0)

    count = ghosts(2 * levels)[0]
    spread = count
    for m in range(SPAN):
        spread = jnp.where((lane >> 3) == m, roll(count, 8 * m + 4, 1), spread)
    edge_out[4 * groups] = spread
    for g in range(groups):
        edges = [jnp.zeros(TILE, jnp.float32)] * 4
        for m in range(min(SPAN, levels - SPAN * g)):
            spot = 2 * (SPAN * g + m)
            window = (lane >> 3) == m
            for f, cells in enumerate((*ghosts(spot), *ghosts(spot + 1))):
                edges[f] = jnp.where(window, roll(cells, 8 * m + 4, 1), edges[f])
        for f in range(4):
            edge_out[f * groups + g] = edges[f]


def step_kernel(
    flags, thermal, salty, east_in, north_in, mixing, count_in,
    first, second, fold, corner_first, corner_second, pack, from_west, from_east, edges,
    thermal_out, salty_out,
    feed, flow_feed, ratio, solved, sent,
):
    levels = thermal.shape[0]
    groups = -(-levels // SPAN)
    row, lane = iotas()
    natural = (row >> 2) == flags[0]
    is_top = (flags[1] + 0 * row) == 1
    top_row = (row == 7) & is_top
    top_ghost = (row < 4) & is_top
    low = (lane & 7) < 4
    at_west = (lane & 7) == 3

    def ghost_pair(a, b):
        return (
            jnp.where(natural, b, a),
            roll(jnp.where(natural, a, b), 4, 0),
        )

    def faces_north(n_m, n_g):
        n_up = roll(n_g, 7, 0)
        return (
            jnp.where(top_row, 0.5 * (n_m + n_up), n_m),
            jnp.where(top_ghost, n_up, n_g),
        )

    def ghosts(spot):
        return ghost_pair(jnp.where(is_top, fold[spot], first[spot]), second[spot])

    def merged(left, right):
        return jnp.where(at_west, left, roll(right, 126, 1))

    def sides(own_m, own_g, spot, beside_g):
        return (
            (
                jnp.where(low, from_west[spot], own_m),
                jnp.where(low, beside_g, own_g),
            ),
            (
                jnp.where(low, own_m, from_east[spot]),
                jnp.where(low, own_g, beside_g),
            ),
        )

    ghost_count = ghosts(2 * levels)[0]
    counts = sides(
        pack[4 * groups],
        edges[4 * groups],
        4 * groups,
        ghost_pair(corner_first[2 * groups], corner_second[2 * groups])[0],
    )
    count_feed = [merged(counts[0][i], counts[1][i]) for i in range(2)]
    for g in range(groups):
        level = (SPAN * g + (lane >> 3)).astype(jnp.float32)
        beside_g = [
            cells
            for i in range(2)
            for cells in ghost_pair(corner_first[2 * g + i], corner_second[2 * g + i])
        ]
        fields = [
            sides(pack[f * groups + g], edges[f * groups + g], f * groups + g, beside_g[f])
            for f in range(4)
        ]
        states = []
        flows = []
        for side in range(2):
            (t_m, t_g), (s_m, s_g), (e_m, e_g), (n_m, n_g) = (field[side] for field in fields)
            c_m, c_g = counts[side]
            up = northward(c_m, c_g, row)
            down = southward(c_m, c_g, row)
            raw_g = e_g
            e_g = jnp.where(top_ghost, roll(e_g, 127, 1), e_g)
            face_n = faces_north(n_m, n_g)
            face_s = southward(face_n[0], face_n[1], row)
            terms = []
            for i, (c, e) in enumerate(((c_m, e_m), (c_g, e_g))):
                limits = (
                    jnp.minimum(c, roll(c, 127, 1)),
                    jnp.minimum(c, roll(c, 1, 1)),
                    jnp.minimum(c, up[i]),
                    jnp.minimum(c, down[i]),
                )
                terms.append(
                    coefficients(e, roll(e, 1, 1), face_n[i], face_s[i], limits, level)
                )
            flows.append((e_m, e_g, raw_g))
            line = []
            for pair in ((t_m, t_g), (s_m, s_g)):
                pair = [
                    jnp.where(level < c, cells, 0.0) for cells, c in zip(pair, (c_m, c_g))
                ]
                track = [pair]
                for _ in range(SPLIT_PASSES - 1):
                    above = northward(pair[0], pair[1], row)
                    below = southward(pair[0], pair[1], row)
                    pair = [
                        apply(c, roll(c, 127, 1), roll(c, 1, 1), above[i], below[i], terms[i])
                        for i, c in enumerate(pair)
                    ]
                    track.append(pair)
                line.append(track)
            states.append(line)
        flow_feed[g] = merged(flows[0][0], flows[1][0])
        flow_feed[groups + g] = merged(flows[0][1], flows[1][2])
        for step in range(SPLIT_PASSES):
            for f in range(2):
                for i in range(2):
                    feed[((step * 2 + f) * 2 + i) * groups + g] = merged(
                        states[0][f][step][i], states[1][f][step][i]
                    )

    first_lane = lane == 0
    last_lane = lane == 127

    def eastward(c, beside):
        return jnp.where(last_lane, beside, roll(c, 127, 1))

    def westward(c, beside):
        return jnp.where(first_lane, beside, roll(c, 1, 1))

    count = (
        count_in[...],
        ghost_count,
    )
    count_beside = [roll(cells, 125, 1) for cells in count_feed]
    up = northward(count[0], count[1], row)
    down = southward(count[0], count[1], row)
    limits = [
        (
            jnp.minimum(count[i], eastward(count[i], count_beside[i])),
            jnp.minimum(count[i], westward(count[i], count_beside[i])),
            jnp.minimum(count[i], up[i]),
            jnp.minimum(count[i], down[i]),
        )
        for i in range(2)
    ]

    def prepare(k):
        g = k >> 4
        shift = (125 - 8 * (k & 15)) & 127
        level = k.astype(jnp.float32)
        t_g, s_g = ghosts(2 * k)
        e_g, n_g = ghosts(2 * k + 1)
        e_m, n_m = east_in[k], north_in[k]
        beside = [roll(flow_feed[i * groups + g], shift, 1) for i in range(2)]
        e_g = jnp.where(top_ghost, eastward(e_g, beside[1]), e_g)
        face_e = (e_m, e_g)
        face_w = [westward(face_e[i], beside[i]) for i in range(2)]
        face_n = faces_north(n_m, n_g)
        face_s = southward(face_n[0], face_n[1], row)
        terms = [
            coefficients(face_e[i], face_w[i], face_n[i], face_s[i], limits[i], level)
            for i in range(2)
        ]
        states = [
            [jnp.where(level < c, cells, 0.0) for cells, c in zip(pair, count)]
            for pair in ((thermal[k], t_g), (salty[k], s_g))
        ]
        open_e, open_w, open_n, open_s = (level < limit for limit in limits[0])
        outflow = (jnp.where(open_e, face_e[0], 0.0) - jnp.where(open_w, face_w[0], 0.0)) + (
            jnp.where(open_n, face_n[0], 0.0) - jnp.where(open_s, face_s[0], 0.0)
        )
        inner = k > 0
        spread = jnp.where(
            (level < count[0]) & inner, mixing[jnp.maximum(k - 1, 0)], 0.0
        )
        return g, shift, terms, states, outflow, inner, spread

    def advance(step, g, shift, terms, states):
        moved_states = []
        for f, pair in enumerate(states):
            above = northward(pair[0], pair[1], row)
            below = southward(pair[0], pair[1], row)
            moved = []
            for i, c in enumerate(pair):
                if step == SPLIT_PASSES - 1 and i == 1:
                    continue
                near = roll(feed[((step * 2 + f) * 2 + i) * groups + g], shift, 1)
                moved.append(
                    apply(c, eastward(c, near), westward(c, near), above[i], below[i], terms[i])
                )
            moved_states.append(moved)
        return moved_states

    def some_levels(bottom, number, carry):
        total, gain_up, gain_down, share, value_t, value_s = carry
        rows = [bottom - u for u in range(number)]
        ready = [prepare(k) for k in rows]
        states = [r[3] for r in ready]
        for step in range(SPLIT_PASSES):
            states = [advance(step, *r[:3], state) for r, state in zip(ready, states)]
        for k, r, state in zip(rows, ready, states):
            outflow, inner, spread = r[4:]
            total = total + outflow
            transport = jnp.where(inner, -float(SPLIT_PASSES) * total, 0.0)
            new_down = jnp.maximum(transport, 0.0) + spread
            new_up = spread - jnp.minimum(transport, 0.0)
            pivot = (1.0 + gain_up + new_down) - gain_down * share
            inverse = 1.0 / pivot
            share = new_up * inverse
            value_t = (state[0][0] + gain_down * value_t) * inverse
            value_s = (state[1][0] + gain_down * value_s) * inverse
            gain_up, gain_down = new_up, new_down
            ratio[k] = share
            solved[0, k] = value_t
            solved[1, k] = value_s
        return total, gain_up, gain_down, share, value_t, value_s

    carry = (jnp.zeros(TILE, jnp.float32),) * 6
    for end, start, together in ((levels, SPAN, BATCH[0]), (SPAN, 0, BATCH[1])):
        carry = lax.fori_loop(
            0,
            (end - start) // together,
            lambda i, c, end=end, together=together: some_levels(
                end - 1 - together * i, together, c
            ),
            carry,
        )

    t, s = solved[0, 0], solved[1, 0]
    copies = []
    for start in range(0, levels, CHUNK):
        end = min(start + CHUNK, levels)
        for k in range(max(start, 1), end):
            part = ratio[k]
            t = solved[0, k] + part * t
            s = solved[1, k] + part * s
            solved[0, k] = t
            solved[1, k] = s
        part = pl.ds(start, end - start)
        for i, target in enumerate((thermal_out, salty_out)):
            copies.append(
                pltpu.make_async_copy(
                    solved.at[i, part], target.at[part], sent.at[start // CHUNK, i]
                )
            )
            copies[-1].start()
    for copy in copies:
        copy.wait()


def call(kernel, shapes, scratch=(), flags=None, direct=0, out=pltpu.VMEM):
    inner = pl.BlockSpec(memory_space=pltpu.VMEM)
    outer = pl.BlockSpec(memory_space=pltpu.HBM)

    def run(*arrays):
        return pl.pallas_call(
            kernel,
            out_shape=tuple(jax.ShapeDtypeStruct(shape, jnp.float32) for shape in shapes),
            in_specs=[pl.BlockSpec(memory_space=pltpu.SMEM)]
            + [outer] * direct
            + [inner] * (len(arrays) - direct),
            out_specs=tuple(pl.BlockSpec(memory_space=out) for _ in shapes),
            scratch_shapes=list(scratch),
            compiler_params=pltpu.CompilerParams(vmem_limit_bytes=32 << 20),
        )(flags, *arrays)

    return run


def routes(lat_count, lon_count):
    first, second, fold = [], [], []
    for lat in range(lat_count):
        even = (lat_count - 1 - lat) % 2 == 0
        for lon in range(lon_count):
            here = lon * lat_count + lat
            if lat == lat_count - 1:
                fold.append((here, (lon_count - 1 - lon) * lat_count + lat))
            else:
                (first if even else second).append((here, here + 1))
            if lat > 0:
                (second if even else first).append((here, here - 1))
    return first, second, fold


def shards(
    thermal_anomaly,
    saltiness_anomaly,
    zonal_volume_flux,
    meridional_volume_flux,
    vertical_diffusion_factor,
    friction_factor,
    seawater_indicator,
    water_layer_depth,
):
    lat_count, lon_count = lax.axis_size("lat"), lax.axis_size("lon")
    lat = lax.axis_index("lat")
    levels = thermal_anomaly.shape[0]
    groups = -(-levels // SPAN)
    above = lat_count - 1 - lat
    flags = jnp.stack([1 - above % 2, (above == 0).astype(jnp.int32)]).astype(jnp.int32)
    field = (levels,) + TILE
    packed = (4 * groups + 1,) + TILE
    message = (2 * levels + 1,) + TILE
    corner = (2 * groups + 1,) + TILE

    east, north, count, pack, first, second = call(
        pack_kernel,
        (field, field, TILE, packed, message, message),
        (
            pltpu.VMEM((5,) + field, jnp.float32),
            pltpu.VMEM((2,) + TILE, jnp.int32),
            pltpu.SemaphoreType.DMA((groups + 1, 5)),
        ),
        flags=flags,
        direct=7,
    )(
        *(
            pltpu.with_memory_space_constraint(field_in, pltpu.HBM)
            for field_in in (
                thermal_anomaly,
                saltiness_anomaly,
                zonal_volume_flux,
                meridional_volume_flux,
                friction_factor,
                seawater_indicator,
                water_layer_depth,
            )
        )
    )
    first_route, second_route, fold_route = routes(lat_count, lon_count)
    both = ("lon", "lat")
    message_first = lax.ppermute(first, both, first_route)
    second = lax.ppermute(second, both, second_route)
    ring = [(i, (i + 1) % lon_count) for i in range(lon_count)]
    from_west = lax.ppermute(pack, "lon", ring)
    from_east = lax.ppermute(pack, "lon", [(b, a) for a, b in ring])
    corner_first, corner_second, fold = call(
        functools.partial(corner_kernel, groups), (corner, corner, message), flags=flags
    )(from_west, from_east, first)
    fold = lax.ppermute(fold, both, fold_route)
    corner_first = lax.ppermute(corner_first, both, first_route + fold_route)
    corner_second = lax.ppermute(corner_second, both, second_route)
    (edges,) = call(edge_kernel, (packed,), flags=flags)(message_first, second, fold)
    return call(
        step_kernel,
        (field, field),
        (
            pltpu.VMEM((16 * groups,) + TILE, jnp.float32),
            pltpu.VMEM((2 * groups,) + TILE, jnp.float32),
            pltpu.VMEM(field, jnp.float32),
            pltpu.VMEM((2,) + field, jnp.float32),
            pltpu.SemaphoreType.DMA((-(-levels // CHUNK), 2)),
        ),
        flags=flags,
        out=pltpu.HBM,
    )(
        thermal_anomaly, saltiness_anomaly, east, north, vertical_diffusion_factor, count,
        message_first, second, fold, corner_first, corner_second, pack, from_west, from_east,
        edges,
    )


def solution(mesh):
    cells = P(None, "lat", "lon")
    columns = P("lat", "lon")
    return jax.shard_map(
        shards,
        mesh=mesh,
        in_specs=(cells,) * 6 + (columns,) * 2,
        out_specs=(cells, cells),
        check_vma=False,
    )
```

```python
import functools

import jax
import jax.numpy as jnp
from jax import lax
from jax.experimental import pallas as pl
from jax.experimental.pallas import tpu as pltpu
from jax.sharding import PartitionSpec as P

SPLIT_PASSES = 4
DIFFUSE = 0.05
TILE = (8, 128)
SPAN = 16
BATCH = 10, 8
CHUNK = 12


def iotas():
    return (
        lax.broadcasted_iota(jnp.int32, TILE, 0),
        lax.broadcasted_iota(jnp.int32, TILE, 1),
    )


def roll(cells, shift, axis):
    return pltpu.roll(cells, shift, axis)


def flip_rows(cells, row):
    for bit in (1, 2, 4):
        cells = jnp.where((row & bit) != 0, roll(cells, bit, 0), roll(cells, 8 - bit, 0))
    return cells


def flip(cells, row, lanes):
    return flip_rows(jnp.take_along_axis(cells, lanes, axis=1), row)


def shared_tiles(t, s, e, n, natural):
    s4, n4 = roll(s, 4, 0), roll(n, 4, 0)
    return jnp.where(natural, t, s4), jnp.where(natural, e, n4)


def pack_kernel(
    flags, thermal, salty, zonal, meridional, friction, indicator, depth,
    east_out, north_out, count_out, pack_out, first_out, second_out, *rest,
):
    *fold_outs, held, columns, arrived = rest
    levels = thermal.shape[0]
    groups = -(-levels // SPAN)
    row, lane = iotas()
    natural = (row >> 2) == flags[0]
    other = (row >> 2) != flags[0]
    flat = [
        pltpu.make_async_copy(source, columns.at[i], arrived.at[groups, i])
        for i, source in enumerate((indicator, depth))
    ]
    for copy in flat:
        copy.start()
    sources = (thermal, salty, zonal, meridional, friction)
    copies = {}
    for g in reversed(range(groups)):
        part = pl.ds(SPAN * g, min(SPAN, levels - SPAN * g))
        copies[g] = [
            pltpu.make_async_copy(source.at[part], held.at[f, part], arrived.at[g, f])
            for f, source in enumerate(sources)
        ]
        for copy in copies[g]:
            copy.start()
    for copy in flat:
        copy.wait()
    count = jnp.where(columns[0] == 1, columns[1], 0).astype(jnp.float32)
    count_out[...] = count
    top_spot = 2 * levels
    first_out[top_spot] = count
    second_out[top_spot] = count
    spread = count
    for m in range(SPAN):
        spread = jnp.where((lane >> 3) == m, roll(count, 8 * m + 4, 1), spread)
    pack_out[4 * groups] = spread

    for g in reversed(range(groups)):
        here = min(SPAN, levels - SPAN * g)
        together = here // 2
        for copy in copies[g]:
            copy.wait()

        def pack_levels(index, packs, g=g, together=together):
            packs = list(packs)
            for u in range(together):
                m = together * index + u
                k = SPAN * g + m
                window = (lane >> 3) == m
                t, s = held[0, k], held[1, k]
                ease = 1.0 / (1.0 + held[4, k])
                e, n = held[2, k] * ease, held[3, k] * ease
                east_out[k] = e
                north_out[k] = n
                first_out[2 * k], first_out[2 * k + 1] = shared_tiles(t, s, e, n, natural)
                second_out[2 * k], second_out[2 * k + 1] = shared_tiles(t, s, e, n, other)
                for f, cells in enumerate((t, s, e, n)):
                    packs[f] = jnp.where(window, roll(cells, 8 * m + 4, 1), packs[f])
            return tuple(packs)

        blank = jnp.zeros(TILE, jnp.float32)
        packs = lax.fori_loop(0, 2, pack_levels, (blank,) * 4)
        for f in range(4):
            pack_out[f * groups + g] = packs[f]

    @pl.when(flags[1] == 1)
    def _():
        lanes = 127 - lane
        start = 0
        for fold_out in fold_outs:
            whole = fold_out.shape[0] // 2 * 2

            def some_tiles(index, carry, start=start, half=whole // 2, fold_out=fold_out):
                for u in range(half):
                    spot = half * index + u
                    tile = flip(first_out[start + spot], row, lanes)
                    fold_out[spot] = jnp.where((start + spot) % 2 == 1, -tile, tile)
                return carry

            lax.fori_loop(0, 2, some_tiles, 0)
            for spot in range(whole, fold_out.shape[0]):
                fold_out[spot] = flip(first_out[start + spot], row, lanes)
            start += fold_out.shape[0]


def corner_kernel(
    groups, flags, from_west, from_east, first_out, second_out
):
    row, lane = iotas()
    natural = (row >> 2) == flags[0]
    other = (row >> 2) != flags[0]
    low = (lane & 7) < 4

    def beside(spot):
        return jnp.where(low, from_west[spot], from_east[spot])

    tiles = []
    for g in range(groups):
        fields = [beside(f * groups + g) for f in range(4)]
        tiles += shared_tiles(*fields, natural)
        second_out[2 * g], second_out[2 * g + 1] = shared_tiles(*fields, other)
    tiles.append(beside(4 * groups))
    second_out[2 * groups] = tiles[-1]
    for spot, tile in enumerate(tiles):
        first_out[spot] = tile

    @pl.when(flags[1] == 1)
    def _():
        for spot, tile in enumerate(tiles):
            tile = flip(tile, row, lane ^ 7)
            first_out[spot] = -tile if spot % 2 == 1 else tile


def folded(folds, spot):
    near, far = folds
    size = near.shape[0]
    if isinstance(spot, int):
        return near[spot] if spot < size else far[spot - size]
    return jnp.where(
        spot < size, near[jnp.minimum(spot, size - 1)], far[jnp.maximum(spot - size, 0)]
    )


def northward(m, g, row):
    m, g = roll(m, 7, 0), roll(g, 7, 0)
    return jnp.where(row == 7, g, m), jnp.where(row == 7, m, g)


def southward(m, g, row):
    m, g = roll(m, 1, 0), roll(g, 1, 0)
    return jnp.where(row == 0, g, m), jnp.where(row == 0, m, g)


def coefficients(east, west, north, south, limits, level):
    open_east, open_west, open_north, open_south = (level < limit for limit in limits)
    leave_east = jnp.where(open_east, DIFFUSE + jnp.maximum(east, 0.0), 0.0)
    from_east = jnp.where(open_east, DIFFUSE - jnp.minimum(east, 0.0), 0.0)
    from_west = jnp.where(open_west, DIFFUSE + jnp.maximum(west, 0.0), 0.0)
    leave_west = jnp.where(open_west, DIFFUSE - jnp.minimum(west, 0.0), 0.0)
    leave_north = jnp.where(open_north, DIFFUSE + jnp.maximum(north, 0.0), 0.0)
    from_north = jnp.where(open_north, DIFFUSE - jnp.minimum(north, 0.0), 0.0)
    from_south = jnp.where(open_south, DIFFUSE + jnp.maximum(south, 0.0), 0.0)
    leave_south = jnp.where(open_south, DIFFUSE - jnp.minimum(south, 0.0), 0.0)
    stay = 1.0 - ((leave_east + leave_west) + (leave_north + leave_south))
    return stay, from_east, from_west, from_north, from_south


def apply(c, east, west, north, south, terms):
    stay, from_east, from_west, from_north, from_south = terms
    return (stay * c + (from_east * east + from_west * west)) + (
        from_north * north + from_south * south
    )


def edge_kernel(flags, first, second, near, far, edge_out):
    levels = first.shape[0] // 2
    groups = -(-levels // SPAN)
    row, lane = iotas()
    natural = (row >> 2) == flags[0]
    is_top = (flags[1] + 0 * row) == 1

    def ghosts(spot):
        a = jnp.where(is_top, folded((near, far), spot), first[spot])
        b = second[spot]
        return jnp.where(natural, b, a), roll(jnp.where(natural, a, b), 4, 0)

    count = ghosts(2 * levels)[0]
    spread = count
    for m in range(SPAN):
        spread = jnp.where((lane >> 3) == m, roll(count, 8 * m + 4, 1), spread)
    edge_out[4 * groups] = spread
    for g in range(groups):
        edges = [jnp.zeros(TILE, jnp.float32)] * 4
        for m in range(min(SPAN, levels - SPAN * g)):
            spot = 2 * (SPAN * g + m)
            window = (lane >> 3) == m
            for f, cells in enumerate((*ghosts(spot), *ghosts(spot + 1))):
                edges[f] = jnp.where(window, roll(cells, 8 * m + 4, 1), edges[f])
        for f in range(4):
            edge_out[f * groups + g] = edges[f]


def step_kernel(
    flags, thermal, salty, east_in, north_in, mixing, count_in,
    first, second, near, far, corner_first, corner_second, pack, from_west, from_east, edges,
    thermal_out, salty_out,
    feed, flow_feed, ratio, solved, sent,
):
    levels = thermal.shape[0]
    groups = -(-levels // SPAN)
    row, lane = iotas()
    natural = (row >> 2) == flags[0]
    is_top = (flags[1] + 0 * row) == 1
    top_row = (row == 7) & is_top
    top_ghost = (row < 4) & is_top
    low = (lane & 7) < 4
    at_west = (lane & 7) == 3

    def ghost_pair(a, b):
        return (
            jnp.where(natural, b, a),
            roll(jnp.where(natural, a, b), 4, 0),
        )

    def faces_north(n_m, n_g):
        n_up = roll(n_g, 7, 0)
        return (
            jnp.where(top_row, 0.5 * (n_m + n_up), n_m),
            jnp.where(top_ghost, n_up, n_g),
        )

    def ghosts(spot):
        return ghost_pair(
            jnp.where(is_top, folded((near, far), spot), first[spot]), second[spot]
        )

    def merged(left, right):
        return jnp.where(at_west, left, roll(right, 126, 1))

    def sides(own_m, own_g, spot, beside_g):
        return (
            (
                jnp.where(low, from_west[spot], own_m),
                jnp.where(low, beside_g, own_g),
            ),
            (
                jnp.where(low, own_m, from_east[spot]),
                jnp.where(low, own_g, beside_g),
            ),
        )

    ghost_count = ghosts(2 * levels)[0]
    counts = sides(
        pack[4 * groups],
        edges[4 * groups],
        4 * groups,
        ghost_pair(corner_first[2 * groups], corner_second[2 * groups])[0],
    )
    count_feed = [merged(counts[0][i], counts[1][i]) for i in range(2)]
    for g in range(groups):
        level = (SPAN * g + (lane >> 3)).astype(jnp.float32)
        beside_g = [
            cells
            for i in range(2)
            for cells in ghost_pair(corner_first[2 * g + i], corner_second[2 * g + i])
        ]
        fields = [
            sides(pack[f * groups + g], edges[f * groups + g], f * groups + g, beside_g[f])
            for f in range(4)
        ]
        states = []
        flows = []
        for side in range(2):
            (t_m, t_g), (s_m, s_g), (e_m, e_g), (n_m, n_g) = (field[side] for field in fields)
            c_m, c_g = counts[side]
            up = northward(c_m, c_g, row)
            down = southward(c_m, c_g, row)
            raw_g = e_g
            e_g = jnp.where(top_ghost, roll(e_g, 127, 1), e_g)
            face_n = faces_north(n_m, n_g)
            face_s = southward(face_n[0], face_n[1], row)
            terms = []
            for i, (c, e) in enumerate(((c_m, e_m), (c_g, e_g))):
                limits = (
                    jnp.minimum(c, roll(c, 127, 1)),
                    jnp.minimum(c, roll(c, 1, 1)),
                    jnp.minimum(c, up[i]),
                    jnp.minimum(c, down[i]),
                )
                terms.append(
                    coefficients(e, roll(e, 1, 1), face_n[i], face_s[i], limits, level)
                )
            flows.append((e_m, e_g, raw_g))
            line = []
            for pair in ((t_m, t_g), (s_m, s_g)):
                pair = [
                    jnp.where(level < c, cells, 0.0) for cells, c in zip(pair, (c_m, c_g))
                ]
                track = [pair]
                for _ in range(SPLIT_PASSES - 1):
                    above = northward(pair[0], pair[1], row)
                    below = southward(pair[0], pair[1], row)
                    pair = [
                        apply(c, roll(c, 127, 1), roll(c, 1, 1), above[i], below[i], terms[i])
                        for i, c in enumerate(pair)
                    ]
                    track.append(pair)
                line.append(track)
            states.append(line)
        flow_feed[g] = merged(flows[0][0], flows[1][0])
        flow_feed[groups + g] = merged(flows[0][1], flows[1][2])
        for step in range(SPLIT_PASSES):
            for f in range(2):
                for i in range(2):
                    feed[((step * 2 + f) * 2 + i) * groups + g] = merged(
                        states[0][f][step][i], states[1][f][step][i]
                    )

    first_lane = lane == 0
    last_lane = lane == 127

    def eastward(c, beside):
        return jnp.where(last_lane, beside, roll(c, 127, 1))

    def westward(c, beside):
        return jnp.where(first_lane, beside, roll(c, 1, 1))

    count = (
        count_in[...],
        ghost_count,
    )
    count_beside = [roll(cells, 125, 1) for cells in count_feed]
    up = northward(count[0], count[1], row)
    down = southward(count[0], count[1], row)
    limits = [
        (
            jnp.minimum(count[i], eastward(count[i], count_beside[i])),
            jnp.minimum(count[i], westward(count[i], count_beside[i])),
            jnp.minimum(count[i], up[i]),
            jnp.minimum(count[i], down[i]),
        )
        for i in range(2)
    ]

    def prepare(k):
        g = k >> 4
        shift = (125 - 8 * (k & 15)) & 127
        level = k.astype(jnp.float32)
        t_g, s_g = ghosts(2 * k)
        e_g, n_g = ghosts(2 * k + 1)
        e_m, n_m = east_in[k], north_in[k]
        beside = [roll(flow_feed[i * groups + g], shift, 1) for i in range(2)]
        e_g = jnp.where(top_ghost, eastward(e_g, beside[1]), e_g)
        face_e = (e_m, e_g)
        face_w = [westward(face_e[i], beside[i]) for i in range(2)]
        face_n = faces_north(n_m, n_g)
        face_s = southward(face_n[0], face_n[1], row)
        terms = [
            coefficients(face_e[i], face_w[i], face_n[i], face_s[i], limits[i], level)
            for i in range(2)
        ]
        states = [
            [jnp.where(level < c, cells, 0.0) for cells, c in zip(pair, count)]
            for pair in ((thermal[k], t_g), (salty[k], s_g))
        ]
        open_e, open_w, open_n, open_s = (level < limit for limit in limits[0])
        outflow = (jnp.where(open_e, face_e[0], 0.0) - jnp.where(open_w, face_w[0], 0.0)) + (
            jnp.where(open_n, face_n[0], 0.0) - jnp.where(open_s, face_s[0], 0.0)
        )
        inner = k > 0
        spread = jnp.where(
            (level < count[0]) & inner, mixing[jnp.maximum(k - 1, 0)], 0.0
        )
        return g, shift, terms, states, outflow, inner, spread

    def advance(step, g, shift, terms, states):
        moved_states = []
        for f, pair in enumerate(states):
            above = northward(pair[0], pair[1], row)
            below = southward(pair[0], pair[1], row)
            moved = []
            for i, c in enumerate(pair):
                if step == SPLIT_PASSES - 1 and i == 1:
                    continue
                near = roll(feed[((step * 2 + f) * 2 + i) * groups + g], shift, 1)
                moved.append(
                    apply(c, eastward(c, near), westward(c, near), above[i], below[i], terms[i])
                )
            moved_states.append(moved)
        return moved_states

    def some_levels(bottom, number, carry):
        total, gain_up, gain_down, share, value_t, value_s = carry
        rows = [bottom - u for u in range(number)]
        ready = [prepare(k) for k in rows]
        states = [r[3] for r in ready]
        for step in range(SPLIT_PASSES):
            states = [advance(step, *r[:3], state) for r, state in zip(ready, states)]
        for k, r, state in zip(rows, ready, states):
            outflow, inner, spread = r[4:]
            total = total + outflow
            transport = jnp.where(inner, -float(SPLIT_PASSES) * total, 0.0)
            new_down = jnp.maximum(transport, 0.0) + spread
            new_up = spread - jnp.minimum(transport, 0.0)
            pivot = (1.0 + gain_up + new_down) - gain_down * share
            inverse = 1.0 / pivot
            share = new_up * inverse
            value_t = (state[0][0] + gain_down * value_t) * inverse
            value_s = (state[1][0] + gain_down * value_s) * inverse
            gain_up, gain_down = new_up, new_down
            ratio[k] = share
            solved[0, k] = value_t
            solved[1, k] = value_s
        return total, gain_up, gain_down, share, value_t, value_s

    carry = (jnp.zeros(TILE, jnp.float32),) * 6
    for end, start, together in ((levels, SPAN, BATCH[0]), (SPAN, 0, BATCH[1])):
        carry = lax.fori_loop(
            0,
            (end - start) // together,
            lambda i, c, end=end, together=together: some_levels(
                end - 1 - together * i, together, c
            ),
            carry,
        )

    t, s = solved[0, 0], solved[1, 0]
    copies = []
    for start in range(0, levels, CHUNK):
        end = min(start + CHUNK, levels)
        for k in range(max(start, 1), end):
            part = ratio[k]
            t = solved[0, k] + part * t
            s = solved[1, k] + part * s
            solved[0, k] = t
            solved[1, k] = s
        part = pl.ds(start, end - start)
        for i, target in enumerate((thermal_out, salty_out)):
            copies.append(
                pltpu.make_async_copy(
                    solved.at[i, part], target.at[part], sent.at[start // CHUNK, i]
                )
            )
            copies[-1].start()
    for copy in copies:
        copy.wait()


def call(kernel, shapes, scratch=(), flags=None, direct=0, out=pltpu.VMEM):
    inner = pl.BlockSpec(memory_space=pltpu.VMEM)
    outer = pl.BlockSpec(memory_space=pltpu.HBM)

    def run(*arrays):
        return pl.pallas_call(
            kernel,
            out_shape=tuple(jax.ShapeDtypeStruct(shape, jnp.float32) for shape in shapes),
            in_specs=[pl.BlockSpec(memory_space=pltpu.SMEM)]
            + [outer] * direct
            + [inner] * (len(arrays) - direct),
            out_specs=tuple(pl.BlockSpec(memory_space=out) for _ in shapes),
            scratch_shapes=list(scratch),
            compiler_params=pltpu.CompilerParams(vmem_limit_bytes=32 << 20),
        )(flags, *arrays)

    return run


def routes(lat_count, lon_count):
    first, second, fold = [], [], []
    for lat in range(lat_count):
        even = (lat_count - 1 - lat) % 2 == 0
        for lon in range(lon_count):
            here = lon * lat_count + lat
            if lat == lat_count - 1:
                fold.append((here, (lon_count - 1 - lon) * lat_count + lat))
            else:
                (first if even else second).append((here, here + 1))
            if lat > 0:
                (second if even else first).append((here, here - 1))
    return first, second, fold


def shards(
    thermal_anomaly,
    saltiness_anomaly,
    zonal_volume_flux,
    meridional_volume_flux,
    vertical_diffusion_factor,
    friction_factor,
    seawater_indicator,
    water_layer_depth,
):
    lat_count, lon_count = lax.axis_size("lat"), lax.axis_size("lon")
    lat = lax.axis_index("lat")
    levels = thermal_anomaly.shape[0]
    groups = -(-levels // SPAN)
    above = lat_count - 1 - lat
    flags = jnp.stack([1 - above % 2, (above == 0).astype(jnp.int32)]).astype(jnp.int32)
    field = (levels,) + TILE
    packed = (4 * groups + 1,) + TILE
    message = (2 * levels + 1,) + TILE
    pieces = [(size,) + TILE for size in (levels, levels + 1)]
    corner = (2 * groups + 1,) + TILE

    east, north, count, pack, first, second, *folds = call(
        pack_kernel,
        (field, field, TILE, packed, message, message, *pieces),
        (
            pltpu.VMEM((5,) + field, jnp.float32),
            pltpu.VMEM((2,) + TILE, jnp.int32),
            pltpu.SemaphoreType.DMA((groups + 1, 5)),
        ),
        flags=flags,
        direct=7,
    )(
        *(
            pltpu.with_memory_space_constraint(field_in, pltpu.HBM)
            for field_in in (
                thermal_anomaly,
                saltiness_anomaly,
                zonal_volume_flux,
                meridional_volume_flux,
                friction_factor,
                seawater_indicator,
                water_layer_depth,
            )
        )
    )
    first_route, second_route, fold_route = routes(lat_count, lon_count)
    both = ("lon", "lat")
    message_first = lax.ppermute(first, both, first_route)
    second = lax.ppermute(second, both, second_route)
    ring = [(i, (i + 1) % lon_count) for i in range(lon_count)]
    from_west = lax.ppermute(pack, "lon", ring)
    from_east = lax.ppermute(pack, "lon", [(b, a) for a, b in ring])
    near, from_east = lax.optimization_barrier((folds[0], from_east))
    far, from_west = lax.optimization_barrier((folds[1], from_west))
    folds = [lax.ppermute(fold, both, fold_route) for fold in (near, far)]
    corner_first, corner_second = call(
        functools.partial(corner_kernel, groups), (corner, corner), flags=flags
    )(from_west, from_east)
    corner_first = lax.ppermute(corner_first, both, first_route + fold_route)
    corner_second, message_first = lax.optimization_barrier((corner_second, message_first))
    corner_second = lax.ppermute(corner_second, both, second_route)
    (edges,) = call(edge_kernel, (packed,), flags=flags)(message_first, second, *folds)
    return call(
        step_kernel,
        (field, field),
        (
            pltpu.VMEM((16 * groups,) + TILE, jnp.float32),
            pltpu.VMEM((2 * groups,) + TILE, jnp.float32),
            pltpu.VMEM(field, jnp.float32),
            pltpu.VMEM((2,) + field, jnp.float32),
            pltpu.SemaphoreType.DMA((-(-levels // CHUNK), 2)),
        ),
        flags=flags,
        out=pltpu.HBM,
    )(
        thermal_anomaly, saltiness_anomaly, east, north, vertical_diffusion_factor, count,
        message_first, second, *folds, corner_first, corner_second, pack, from_west, from_east,
        edges,
    )


def solution(mesh):
    cells = P(None, "lat", "lon")
    columns = P("lat", "lon")
    return jax.shard_map(
        shards,
        mesh=mesh,
        in_specs=(cells,) * 6 + (columns,) * 2,
        out_specs=(cells, cells),
        check_vma=False,
    )
```
